128 devices in a mesh: slab: 32 (over x, z, y_hi), dp: 4 (over y_lo, core).
Axes of the slice: x: 4, y: 4 (y_hi: 2, y_lo: 2; y = y_hi * 2 + y_lo), z: 4, core: 2. Of those that a mesh axis runs over, the one named last changes fastest.
Arguments:
- field: bfloat16 [4, 64, 32, 64, 512], P('dp', 'slab'), may hold values from -6 to 6
- cotangent: bfloat16 [4, 64, 32, 64, 512], P('dp', 'slab'), may hold values from -6 to 6
- spectral_weight: bfloat16 [96, 16, 16, 32, 64], P('slab'), may hold values from -9 to 9
- point_weight: bfloat16 [32, 32], replicated, may hold values from -1 to 1
- bias_term: float32 [32], replicated, may hold values from -3 to 3
Outputs:
- layer_out: bfloat16 [4, 64, 32, 64, 512], P('dp', 'slab')
- field_grad: bfloat16 [4, 64, 32, 64, 512], P('dp', 'slab')
- weight_grad: float32 [96, 16, 16, 32, 64], P('slab')
The draws below stay inside these ranges and needn't reach their ends.
All inputs are finite; a program needn't handle non-finite values.
Results may differ from the reference program's by a relative error of at most 0.018.
Values may be sent and summed in bfloat16 or wider, within the bound.
No kernel may reach another device: no remote copies, remote signals or barrier semaphores. Data moves between devices by JAX's collectives and lax.ppermute only.
A program may use at most 128 MiB of HBM per device.

```python
import math
from functools import partial
import jax
import jax.numpy as jnp
from jax import lax

X = 64
Y = 64
Z = 32
T_SIZE = 16
C = 32
MX = 16
MY = 16
MZ = 12
MT = 8
ZT = 512
KZT = 96
SAMPLES = 4


def levels(rng, extent, split, least, largest):
    loudness, own = 1.0, jax.random.fold_in(rng, 6)
    for position, blocks in split:
        heights = jnp.exp(jax.random.uniform(jax.random.fold_in(own, position), (blocks,), jnp.float32, least / len(split), largest / len(split)))
        loudness = loudness * jnp.repeat(heights, extent[position] // blocks).reshape([-1 if axis == position else 1 for axis in range(len(extent))])
    return loudness


def noise(key, dims, deviation, most, shards=(), kind=jnp.bfloat16):
    array = jax.random.normal(key, dims, jnp.float32) * deviation
    if len(shards) > 0:
        array = levels(key, dims, shards, -0.22, 0.18) * array
    return jnp.clip(array, min=-most, max=most).astype(kind)


def setup_inputs(seed: int = 0) -> dict:
    seeds = jax.random.split(jax.random.key(seed), 6)
    return {
        "field": noise(seeds[0], (SAMPLES, X, C, Y, ZT), 1.0, 6.0, ((0, 4), (1, 32))),
        "cotangent": noise(seeds[1], (SAMPLES, X, C, Y, ZT), 1.0, 6.0, ((0, 4), (1, 32))),
        "spectral_weight": noise(seeds[2], (KZT, MX, MY, C, 2 * C), 1.5, 9.0, ((0, 32),)),
        "point_weight": noise(seeds[3], (C, C), C ** -0.5, 1.0),
        "bias_term": noise(seeds[4], (C,), 0.5, 3.0, (), jnp.float32),
    }


def signed_freq(index, modes):
    return jnp.where(index < modes // 2, index, index - modes)

def inner_table():
    freq = jnp.arange(MZ * MT, dtype=jnp.int32)
    place = jnp.arange(Z * T_SIZE, dtype=jnp.int32)
    kdepth = (signed_freq(freq // MT, MZ) % Z)[:, None]
    ktime = (freq % MT)[:, None]
    zdepth = (place // T_SIZE)[None, :]
    tlevel = (place % T_SIZE)[None, :]
    counts = kdepth * zdepth % Z * T_SIZE + ktime * tlevel % T_SIZE * Z
    angle = 2.0 * math.pi / (Z * T_SIZE) * (counts % (Z * T_SIZE)).astype(jnp.float32)
    return jnp.stack([jnp.cos(angle), -jnp.sin(angle)]).astype(jnp.bfloat16)

def complex_table(modes, length):
    kpos = (signed_freq(jnp.arange(modes, dtype=jnp.int32), modes) % length)[:, None]
    jpos = jnp.arange(length, dtype=jnp.int32)[None, :]
    angle = 2.0 * math.pi / length * (kpos * jpos % length).astype(jnp.float32)
    cosine = jnp.cos(angle)
    sine = jnp.sin(angle)
    first = jnp.stack([cosine, sine], axis=1)
    second = jnp.stack([-sine, cosine], axis=1)
    return jnp.stack([first, second]).astype(jnp.bfloat16)

def contract(form, left, right):
    return jnp.einsum(form, left.astype(jnp.float32), right.astype(jnp.float32), precision=lax.Precision.HIGHEST)

def analyse(values, inner, middle, outer):
    first = contract('xcyt,pqt->xqpyc', values, inner).astype(jnp.bfloat16)
    second = contract('rkpy,xqpyc->xqrkc', middle, first).astype(jnp.bfloat16)
    return contract('rkpx,xqpyc->qkryc', outer, second)

def synthesise(spectrum, inner, middle, outer):
    first = contract('pkrx,qkpyc->xqryc', outer, spectrum).astype(jnp.bfloat16)
    second = contract('pkry,xqpkc->xqryc', middle, first).astype(jnp.bfloat16)
    return contract('xqpyc,pqt->xcyt', second, inner)

def pairs(grad_spec):
    real_part = grad_spec[..., 0, :, :]
    imag_part = grad_spec[..., 1, :, :]
    first = jnp.concatenate([real_part, imag_part], axis=-1)
    second = jnp.concatenate([imag_part, -real_part], axis=-1)
    return jnp.stack([first, second], axis=-3)

def mixing(spectrum, weights):
    both = contract('qkpyc,qkyco->qkpyo', spectrum, weights)
    real_part = both[:, :, 0, :, :C] - both[:, :, 1, :, C:]
    imag_part = both[:, :, 0, :, C:] + both[:, :, 1, :, :C]
    return jnp.stack([real_part, imag_part], axis=2).astype(jnp.bfloat16)

def one_sample(inputs, upstream, spectral_weight, point_weight, bias_term):
    inner = inner_table()
    middle = complex_table(MY, Y)
    outer = complex_table(MX, X)
    scale = 1.0 / (X * Y * Z * T_SIZE)
    spectrum = analyse(inputs, inner, middle, outer).astype(jnp.bfloat16)
    mixed = mixing(spectrum, spectral_weight)
    spectral = synthesise(mixed, inner, middle, outer) * scale
    linear = contract('oc,xcyt->xoyt', point_weight, inputs)
    preact = spectral + linear + bias_term[None, :, None, None]
    activation = partial(jax.nn.gelu, approximate=True)
    layer_out = activation(preact).astype(jnp.bfloat16)
    pulled = jax.vjp(activation, preact)[1](upstream.astype(preact.dtype))[0]
    grad_pre = pulled.astype(jnp.bfloat16)
    grad_spec = (analyse(grad_pre, inner, middle, outer) * scale).astype(jnp.bfloat16)
    spec_back = contract('qkyco,qkpyo->qkpyc', spectral_weight, pairs(grad_spec)).astype(jnp.bfloat16)
    total = synthesise(spec_back, inner, middle, outer) + contract('oc,xoyt->xcyt', point_weight, grad_pre)
    return (layer_out, total.astype(jnp.bfloat16), spectrum, grad_spec)

def reference(field, cotangent, spectral_weight, point_weight, bias_term):

    def per_sample(inputs):
        return one_sample(inputs[0], inputs[1], spectral_weight, point_weight, bias_term)
    layer_out, field_grad, spectra, grad_spectra = lax.map(per_sample, (field, cotangent))
    weight_grad = contract('sqkpyc,sqkpyo->qkyco', spectra, pairs(grad_spectra))
    return (layer_out, field_grad, weight_grad)
```

```python
import math
from functools import partial

import jax
import jax.numpy as jnp
import numpy as np
from jax import lax
from jax.experimental import pallas as pl
from jax.experimental.pallas import tpu as pltpu
from jax.sharding import PartitionSpec as P

X = 64
Y = 64
Z = 32
T_SIZE = 16
ZT = Z * T_SIZE
C = 32
MX = 16
MY = 16
MZ = 12
MT = 8
NQ = 3
ND = 32
SCALE = 1.0 / (X * Y * Z * T_SIZE)
BF = jnp.bfloat16
F32 = jnp.float32


def signed(modes):
    i = np.arange(modes)
    return np.where(i < modes // 2, i, i - modes)


def inner_np():
    q = np.arange(MZ * MT)
    place = np.arange(ZT)
    kz = (signed(MZ)[q // MT] % Z)[:, None]
    kt = (q % MT)[:, None]
    counts = kz * (place // T_SIZE)[None] % Z * T_SIZE + kt * (place % T_SIZE)[None] % T_SIZE * Z
    angle = 2.0 * math.pi / ZT * (counts % ZT)
    return np.stack([np.cos(angle), -np.sin(angle)]).astype(np.float32)


def complex_np(modes, length):
    k = (signed(modes) % length)[:, None]
    angle = 2.0 * math.pi / length * (k * np.arange(length)[None] % length)
    c, s = np.cos(angle), np.sin(angle)
    return np.stack([np.stack([c, s], 1), np.stack([-s, c], 1)]).astype(np.float32)


def tables():
    inner = inner_np()
    mid = complex_np(MY, Y)
    out = complex_np(MX, X)
    by_owner = inner.reshape(2, ND, NQ, ZT).transpose(0, 2, 1, 3)
    ana_in = by_owner.reshape(192, ZT)
    syn_in = np.zeros((2, 128, ZT), np.float32)
    syn_in[:, :96] = by_owner.reshape(2, 96, ZT)
    syn_in = syn_in.reshape(256, ZT)
    eye8 = np.eye(8, dtype=np.float32)
    ana_mid = np.einsum("rkpy,cd->pcyrkd", mid, eye8).reshape(2, 512, 256)
    syn_mid = np.einsum("pkry,cd->rcypkd", mid, eye8).reshape(1024, 256)
    eye4 = np.eye(4, dtype=np.float32)
    ana_out = np.einsum("rkpsi,gh->grkspih", out.reshape(2, MX, 2, ND, 2), eye4).reshape(128, 512)
    syn_out = out.reshape(2, MX, 2, ND, 2).transpose(2, 4, 3, 0, 1)
    fwd_out = np.repeat(syn_out.reshape(128, 32), 16, axis=1)
    bwd_out = np.repeat(syn_out.reshape(128, 32), 8, axis=1)
    perm = np.zeros((4, MY, 8, MY, 4, 8), np.float32)
    for g in range(4):
        for k in range(MY):
            for c in range(8):
                perm[g, k, c, k, g, c] = 1.0
    perm = perm.reshape(512, 512)
    spread = np.zeros((2, 2, 4, 8, 4, MY, 8), np.float32)
    for g in range(4):
        for c in range(8):
            spread[0, 0, g, c, g, :, c] = 1.0
            spread[1, 1, g, c, g, :, c] = 1.0
    spread = spread.reshape(2, 64, 512)
    fold = np.zeros((2, 8, C, 128), np.float32)
    for o in range(C):
        fold[0, :, o, o] = 1.0
        fold[0, :, o, 96 + o] = -1.0
        fold[1, :, o, 32 + o] = 1.0
        fold[1, :, o, 64 + o] = 1.0
    fold = fold.reshape(2, 256, 128)
    t = dict(
        ana_in=ana_in, syn_in=syn_in, ana_mid=ana_mid, syn_mid=syn_mid, ana_out=ana_out,
        fwd_out=fwd_out, bwd_out=bwd_out, perm=perm, spread=spread, fold=fold,
    )
    return {k: jnp.asarray(v, BF) for k, v in t.items()}


def dot(a, b):
    return lax.dot_general(a, b, (((1,), (0,)), ((), ())), preferred_element_type=F32)


def dot_t(a, b):
    return lax.dot_general(a, b, (((1,), (1,)), ((), ())), preferred_element_type=F32)


def analyse_rows(rows, slot, ana_in, ana_mid, work):
    first = dot_t(ana_in[...], rows).astype(BF)
    second = dot(first[:96], ana_mid[0]) + dot(first[96:], ana_mid[1])
    for qi in range(NQ):
        for r in range(2):
            work[qi, pl.ds(r * 8 + slot, ND, stride=16), :] = second[
                qi * 32 : qi * 32 + 32, r * 128 : r * 128 + 128
            ]


def flush(work, out):
    for qi in range(NQ):
        out[:, qi * 16 : qi * 16 + 16, :] = work[qi].reshape(ND, 16, 128).astype(BF)


def analyse_body(v, ana_in, ana_mid, out, work):
    step = pl.program_id(0)
    analyse_rows(v[...], step, ana_in, ana_mid, work)

    @pl.when(step == 7)
    def _():
        flush(work, out)


def whole(shape):
    return pl.BlockSpec(shape, lambda i: (0,) * len(shape))


def rows_spec():
    return pl.BlockSpec((512, ZT), lambda i: (i, 0))


def analyse(values, t):
    return pl.pallas_call(
        analyse_body,
        grid=(8,),
        in_specs=[rows_spec(), whole((192, ZT)), whole((2, 512, 256))],
        out_specs=whole((ND, 48, 128)),
        out_shape=jax.ShapeDtypeStruct((ND, 48, 128), BF),
        scratch_shapes=[pltpu.VMEM((NQ, 512, 128), F32)],
        name="analyse",
    )(values, t["ana_in"], t["ana_mid"])


def spectrum_rows(got, ana_out, perm, scale):
    parts = dot(ana_out[...], got[...].reshape(512, 128))
    if scale is not None:
        parts = parts * scale
    parts = parts.astype(BF)
    joined = jnp.concatenate([parts[g * 32 : g * 32 + 32] for g in range(4)], axis=1)
    return dot(joined, perm[...])


def mode_mask():
    lane = lax.broadcasted_iota(jnp.int32, (8, 256), 1) // 32
    return lane == lax.broadcasted_iota(jnp.int32, (8, 256), 0)


def scatter_owner(synth, work, out):
    for r in range(2):
        for xi in range(2):
            for g in range(4):
                at = (r * 2 + xi) * 32
                work[pl.ds(r * 8 + xi * 4 + g, ND, stride=16), :] = synth[
                    at : at + 32, g * 128 : g * 128 + 128
                ]
    out[...] = work[...].reshape(ND, 16, 128).astype(BF)


def mix_forward_body(got, w, ana_out, perm, spread, fwd_out, out, spec, srow, mixed, work):
    rows = spectrum_rows(got, ana_out, perm, None)
    spec[...] = rows.astype(BF)
    srow[...] = rows
    mask = mode_mask()
    for kx in range(MX):
        for h in range(2):
            lanes = slice(h * 256, h * 256 + 256)
            real = jnp.where(mask, jnp.broadcast_to(srow[kx : kx + 1, lanes], (8, 256)), 0.0)
            imag = jnp.where(mask, jnp.broadcast_to(srow[16 + kx : 17 + kx, lanes], (8, 256)), 0.0)
            left = jnp.concatenate([real, imag], axis=0).astype(BF)
            at = (kx * 2 + h) * 256
            both = dot(left, w[at : at + 256, :])
            low = both[8:16]
            turned = jnp.concatenate([-low[:, 32:], low[:, :32]], axis=1)
            mixed[kx * 16 + h * 8 : kx * 16 + h * 8 + 8, :] = both[:8] + turned
    values = mixed[...].astype(BF)
    row_ky = lax.broadcasted_iota(jnp.int32, (256, 512), 0) % 16
    lane_ky = lax.broadcasted_iota(jnp.int32, (256, 512), 1) // 8 % 16
    same = row_ky == lane_ky
    wide = [jnp.where(same, dot(values, spread[p]), 0.0).astype(BF) for p in range(2)]
    synth = dot(fwd_out[...], jnp.concatenate(wide, axis=0))
    scatter_owner(synth, work, out)


def squeezed(shape):
    return pl.BlockSpec((None,) + shape, lambda i: (i,) + (0,) * len(shape))


def slot_spec():
    return pl.BlockSpec((ND, 16, 128), lambda i: (0, i, 0))


def mix_forward(got, weights, t):
    return pl.pallas_call(
        mix_forward_body,
        grid=(NQ,),
        in_specs=[
            slot_spec(), squeezed((8192, 64)), whole((128, 512)), whole((512, 512)),
            whole((2, 64, 512)), whole((128, 512)),
        ],
        out_specs=[slot_spec(), squeezed((32, 512))],
        out_shape=[
            jax.ShapeDtypeStruct((ND, 48, 128), BF),
            jax.ShapeDtypeStruct((NQ, 32, 512), BF),
        ],
        scratch_shapes=[
            pltpu.VMEM((32, 512), F32), pltpu.VMEM((256, 64), F32), pltpu.VMEM((512, 128), F32),
        ],
        name="mix_forward",
    )(got, weights, t["ana_out"], t["perm"], t["spread"], t["fwd_out"])


def mix_backward_body(
    got, w, ana_out, perm, fold, bwd_out, out, spec, srow, pair, masked, work
):
    rows = spectrum_rows(got, ana_out, perm, SCALE)
    spec[...] = rows.astype(BF)
    srow[...] = rows
    mask = mode_mask()
    for h in range(2):
        total = None
        for part in range(2):
            lanes = slice(h * 256, h * 256 + 256)
            tall = [
                jnp.where(mask, jnp.broadcast_to(srow[k : k + 1, lanes], (8, 256)), 0.0)
                for k in range(part * 16, part * 16 + 16)
            ]
            one = dot(jnp.concatenate(tall, axis=0).astype(BF), fold[part])
            total = one if total is None else total + one
        pair[h] = total
    for kx in range(MX):
        for h in range(2):
            both = pair[h, kx * 8 : kx * 8 + 8, :]
            left = jnp.concatenate([both[:, :64], both[:, 64:]], axis=0).astype(BF)
            at = (kx * 2 + h) * 256
            full = dot_t(left, w[at : at + 256, :])
            masked[h, kx * 8 : kx * 8 + 8, :] = jnp.where(mask, full[:8], 0.0)
            masked[h, 128 + kx * 8 : 136 + kx * 8, :] = jnp.where(mask, full[8:], 0.0)
    synth = [dot(bwd_out[...], masked[h].astype(BF)).astype(BF) for h in range(2)]
    turned = dot_t(jnp.concatenate(synth, axis=1), perm[...])
    scatter_owner(turned, work, out)


def mix_backward(got, weights, t):
    return pl.pallas_call(
        mix_backward_body,
        grid=(NQ,),
        in_specs=[
            slot_spec(), squeezed((8192, 64)), whole((128, 512)), whole((512, 512)),
            whole((2, 256, 128)), whole((128, 256)),
        ],
        out_specs=[slot_spec(), squeezed((32, 512))],
        out_shape=[
            jax.ShapeDtypeStruct((ND, 48, 128), BF),
            jax.ShapeDtypeStruct((NQ, 32, 512), BF),
        ],
        scratch_shapes=[
            pltpu.VMEM((32, 512), F32), pltpu.VMEM((2, 128, 128), F32),
            pltpu.VMEM((2, 256, 256), F32), pltpu.VMEM((512, 128), F32),
        ],
        name="mix_backward",
    )(got, weights, t["ana_out"], t["perm"], t["fold"], t["bwd_out"])


def unpack(got, have):
    for qi in range(NQ):
        have[qi] = got[:, qi * 16 : qi * 16 + 16, :].reshape(512, 128).astype(F32)


def synthesise_rows(slot, have, syn_mid, syn_in):
    parts = []
    for p in range(2):
        pieces = [have[qi, pl.ds(p * 8 + slot, ND, stride=16), :] for qi in range(NQ)]
        pieces.append(jnp.zeros((ND, 128), F32))
        parts.append(jnp.concatenate(pieces, axis=0).astype(BF))
    both = jnp.concatenate(parts, axis=1)
    tall = dot_t(syn_mid[...], both).astype(BF)
    return dot(jnp.concatenate([tall[:512], tall[512:]], axis=1), syn_in[...])


ROOT = math.sqrt(2.0 / math.pi)
CHUNK = 32


def activate_body(
    got, lin, cot, syn_mid, syn_in, ana_in, ana_mid, act, grad, out, have, spectral, work
):
    step = pl.program_id(0)

    @pl.when(step == 0)
    def _():
        unpack(got, have)

    spectral[...] = synthesise_rows(step, have, syn_mid, syn_in)

    def chunk(i, carry):
        at = pl.ds(pl.multiple_of(i * CHUNK, CHUNK), CHUNK)
        v = spectral[at, :] * SCALE + lin[at, :]
        square = v * v
        half = 0.5 + 0.5 * jnp.tanh(v * (ROOT + (ROOT * 0.044715) * square))
        value = v * half
        slope = half + (value - value * half) * (2.0 * ROOT + (6.0 * ROOT * 0.044715) * square)
        act[at, :] = value.astype(BF)
        grad[at, :] = (cot[at, :].astype(F32) * slope).astype(BF)
        return carry

    lax.fori_loop(0, 512 // CHUNK, chunk, 0)
    analyse_rows(grad[...], step, ana_in, ana_mid, work)

    @pl.when(step == 7)
    def _():
        flush(work, out)


def activate(got, lin, cot, t):
    return pl.pallas_call(
        activate_body,
        grid=(8,),
        in_specs=[
            whole((ND, 48, 128)), rows_spec(), rows_spec(), whole((1024, 256)), whole((256, ZT)),
            whole((192, ZT)), whole((2, 512, 256)),
        ],
        out_specs=[rows_spec(), rows_spec(), whole((ND, 48, 128))],
        out_shape=[
            jax.ShapeDtypeStruct((4096, ZT), BF),
            jax.ShapeDtypeStruct((4096, ZT), BF),
            jax.ShapeDtypeStruct((ND, 48, 128), BF),
        ],
        scratch_shapes=[
            pltpu.VMEM((NQ, 512, 128), F32), pltpu.VMEM((512, ZT), F32), pltpu.VMEM((NQ, 512, 128), F32),
        ],
        name="activate",
    )(got, lin, cot, t["syn_mid"], t["syn_in"], t["ana_in"], t["ana_mid"])


def finish_body(got, lin, syn_mid, syn_in, out, have):
    step = pl.program_id(0)

    @pl.when(step == 0)
    def _():
        unpack(got, have)

    out[...] = (synthesise_rows(step, have, syn_mid, syn_in) + lin[...]).astype(BF)


def finish(got, lin, t):
    return pl.pallas_call(
        finish_body,
        grid=(8,),
        in_specs=[whole((ND, 48, 128)), rows_spec(), whole((1024, 256)), whole((256, ZT))],
        out_specs=rows_spec(),
        out_shape=jax.ShapeDtypeStruct((4096, ZT), BF),
        scratch_shapes=[pltpu.VMEM((NQ, 512, 128), F32)],
        name="finish",
    )(got, lin, t["syn_mid"], t["syn_in"])


def linear_body(v, kron, bias, out):
    out[...] = (dot(kron[...], v[...].reshape(256, ZT)) + bias[...]).reshape(C, 8, ZT)


def linear(values, matrix, bias):
    block = pl.BlockSpec((None, C, 8, ZT), lambda i: (i // 8, 0, i % 8, 0))
    eye = jnp.eye(8, dtype=F32)
    kron = (matrix.astype(F32)[:, None, :, None] * eye[None, :, None, :]).reshape(256, 256)
    return pl.pallas_call(
        linear_body,
        grid=(16,),
        in_specs=[block, whole((256, 256)), whole((256, 1))],
        out_specs=block,
        out_shape=jax.ShapeDtypeStruct((2, C, Y, ZT), F32),
        name="linear",
    )(values, kron.astype(BF), jnp.repeat(bias, 8)[:, None])


def weight_body(*refs):
    specs, grads = refs[:4], refs[4:8]
    fold, out, srow, grow = refs[8:]
    group = pl.program_id(0) % 4

    @pl.when(group == 0)
    def _():
        for s in range(4):
            srow[s] = specs[s][...].astype(F32)
            grow[s] = grads[s][...].astype(F32)

    mask = mode_mask()
    low = lax.broadcasted_iota(jnp.int32, (32, 128), 1) < 64
    blank = jnp.zeros((64, 128), F32)

    def tall(ref, s, p, j, h):
        row = ref[s, pl.ds(p * 16 + group * 4 + j, 1), h * 256 : h * 256 + 256]
        return jnp.where(mask, jnp.broadcast_to(row, (8, 256)), 0.0)

    for h in range(2):
        left = [tall(srow, s, p, j, h) for j in range(4) for p in range(2) for s in range(4)]
        left = jnp.concatenate(left, axis=0).astype(BF)
        pair = None
        for p in range(2):
            rows = [tall(grow, s, p, j, h) for j in range(4) for s in range(4)]
            one = dot(jnp.concatenate(rows, axis=0).astype(BF), fold[p])
            pair = one if pair is None else pair + one
        blocks = []
        for j in range(4):
            here = pair[j * 32 : j * 32 + 32]
            there = jnp.concatenate([here[:, 64:], here[:, :64]], axis=1)
            if j % 2 == 0:
                first, second = jnp.where(low, here, 0.0), jnp.where(low, there, 0.0)
            else:
                first, second = jnp.where(low, 0.0, there), jnp.where(low, 0.0, here)
            piece = jnp.concatenate([first, second], axis=0)
            blocks.append(jnp.concatenate([piece, blank] if j < 2 else [blank, piece], axis=1))
        right = jnp.concatenate(blocks, axis=0).astype(BF)
        grad = lax.dot_general(left, right, (((0,), (0,)), ((), ())), preferred_element_type=F32)
        for j in range(4):
            at = (j * 2 + h) * 256
            out[at : at + 256, :] = grad[:, j * 64 : j * 64 + 64]


def weight_gradient(specs, grads, t):
    rows = pl.BlockSpec((None, 32, 512), lambda i: (i // 4, 0, 0))
    return pl.pallas_call(
        weight_body,
        grid=(NQ * 4,),
        in_specs=[rows] * 8 + [whole((2, 256, 128))],
        out_specs=pl.BlockSpec((None, 2048, 64), lambda i: (i // 4, i % 4, 0)),
        out_shape=jax.ShapeDtypeStruct((NQ, 8192, 64), F32),
        scratch_shapes=[pltpu.VMEM((4, 32, 512), F32), pltpu.VMEM((4, 32, 512), F32)],
        name="weight_gradient",
    )(*specs, *grads, t["fold"])


def exchange(values):
    return lax.all_to_all(values, "slab", split_axis=0, concat_axis=0, tiled=True)


def everyone(values):
    pieces = [values]
    for k in range(1, 4):
        pieces.append(lax.ppermute(values, "dp", [(i, i ^ k) for i in range(4)]))
    return pieces


def per_device(field, cotangent, spectral_weight, point_weight, bias_term):
    t = tables()
    rows = field.reshape(4096, ZT)
    weights = spectral_weight.reshape(NQ, 8192, 64)
    sent = exchange(analyse(rows, t))
    lin = linear(field[0], point_weight, bias_term)
    back, spec = mix_forward(sent, weights, t)
    got = exchange(back)
    specs = everyone(spec)
    act, grad_pre, out = activate(got, lin.reshape(4096, ZT), cotangent.reshape(4096, ZT), t)
    sent = exchange(out)
    lin = linear(grad_pre.reshape(2, C, Y, ZT), point_weight.T, jnp.zeros_like(bias_term))
    back, grad_spec = mix_backward(sent, weights, t)
    got = exchange(back)
    grads = everyone(grad_spec)
    weight_grad = weight_gradient(specs, grads, t).reshape(NQ, MX, MY, C, 2 * C)
    total = finish(got, lin.reshape(4096, ZT), t)
    shape = (1, 2, C, Y, ZT)
    return act.reshape(shape), total.reshape(shape), weight_grad


def solution(mesh):
    placed = (
        P("dp", "slab", None, None, None),
        P("dp", "slab", None, None, None),
        P("slab", None, None, None, None),
        P(),
        P(),
    )
    return jax.shard_map(
        per_device,
        mesh=mesh,
        in_specs=placed,
        out_specs=(
            P("dp", "slab", None, None, None),
            P("dp", "slab", None, None, None),
            P("slab", None, None, None, None),
        ),
        check_vma=False,
    )
```

```python
import math
from functools import partial

import jax
import jax.numpy as jnp
import numpy as np
from jax import lax
from jax.experimental import pallas as pl
from jax.experimental.pallas import tpu as pltpu
from jax.sharding import PartitionSpec as P

X = 64
Y = 64
Z = 32
T_SIZE = 16
ZT = Z * T_SIZE
C = 32
MX = 16
MY = 16
MZ = 12
MT = 8
NQ = 3
ND = 32
SCALE = 1.0 / (X * Y * Z * T_SIZE)
BF = jnp.bfloat16
F32 = jnp.float32


def signed(modes):
    i = np.arange(modes)
    return np.where(i < modes // 2, i, i - modes)


def inner_np():
    q = np.arange(MZ * MT)
    place = np.arange(ZT)
    kz = (signed(MZ)[q // MT] % Z)[:, None]
    kt = (q % MT)[:, None]
    counts = kz * (place // T_SIZE)[None] % Z * T_SIZE + kt * (place % T_SIZE)[None] % T_SIZE * Z
    angle = 2.0 * math.pi / ZT * (counts % ZT)
    return np.stack([np.cos(angle), -np.sin(angle)]).astype(np.float32)


def complex_np(modes, length):
    k = (signed(modes) % length)[:, None]
    angle = 2.0 * math.pi / length * (k * np.arange(length)[None] % length)
    c, s = np.cos(angle), np.sin(angle)
    return np.stack([np.stack([c, s], 1), np.stack([-s, c], 1)]).astype(np.float32)


def tables():
    inner = inner_np()
    mid = complex_np(MY, Y)
    out = complex_np(MX, X)
    depth = np.zeros((2, 128, ZT), np.float32)
    depth[:, :96] = inner.reshape(2, ND, NQ, ZT).transpose(0, 2, 1, 3).reshape(2, 96, ZT)
    depth = depth.reshape(256, ZT)
    middle = np.einsum("rkpy,cd->pcyrkd", mid, np.eye(8, dtype=np.float32)).reshape(1024, 256)
    eye4 = np.eye(4, dtype=np.float32)
    ana_out = np.einsum("rkpsi,gh->grkspih", out.reshape(2, MX, 2, ND, 2), eye4).reshape(128, 512)
    syn_out = out.reshape(2, MX, 2, ND, 2).transpose(2, 4, 3, 0, 1)
    fwd_out = np.repeat(syn_out.reshape(128, 32), 16, axis=1)
    bwd_out = np.repeat(syn_out.reshape(128, 32), 8, axis=1)
    perm = np.zeros((4, MY, 8, MY, 4, 8), np.float32)
    for g in range(4):
        for k in range(MY):
            for c in range(8):
                perm[g, k, c, k, g, c] = 1.0
    perm = perm.reshape(512, 512)
    spread = np.zeros((2, 2, 4, 8, 4, MY, 8), np.float32)
    for g in range(4):
        for c in range(8):
            spread[0, 0, g, c, g, :, c] = 1.0
            spread[1, 1, g, c, g, :, c] = 1.0
    spread = spread.reshape(2, 64, 512)
    fold = np.zeros((2, 8, C, 128), np.float32)
    for o in range(C):
        fold[0, :, o, o] = 1.0
        fold[0, :, o, 96 + o] = -1.0
        fold[1, :, o, 32 + o] = 1.0
        fold[1, :, o, 64 + o] = 1.0
    fold = fold.reshape(2, 256, 128)
    t = dict(
        depth=depth, middle=middle, ana_out=ana_out, fwd_out=fwd_out * SCALE, bwd_out=bwd_out,
        perm=perm, spread=spread, fold=fold,
    )
    return {k: jnp.asarray(v, BF) for k, v in t.items()}


def dot(a, b):
    return lax.dot_general(a, b, (((1,), (0,)), ((), ())), preferred_element_type=F32)


def dot_t(a, b):
    return lax.dot_general(a, b, (((1,), (1,)), ((), ())), preferred_element_type=F32)


def owner_table(depth):
    return jnp.concatenate([depth[0:96, :], depth[128:224, :]], axis=0)


def analyse_rows(rows, slot, table, first):
    part = dot_t(table, rows).astype(BF)
    at = pl.ds(slot * 96, 96) if isinstance(slot, int) else pl.ds(pl.multiple_of(slot * 96, 32), 96)
    first[at, 0:512] = part[:96]
    first[at, 512:1024] = part[96:]


def by_owner(first, middle, out, work):
    second = dot(first[...], middle[...])
    for slot in range(8):
        for qi in range(NQ):
            for r in range(2):
                at = slot * 96 + qi * 32
                work[qi, pl.ds(r * 8 + slot, ND, stride=16), :] = second[
                    at : at + 32, r * 128 : r * 128 + 128
                ]
    for qi in range(NQ):
        out[:, qi * 16 : qi * 16 + 16, :] = work[qi].reshape(ND, 16, 128).astype(BF)


def chunk_copy(src, dst, sem, k):
    at = pl.ds(k * 512, 512)
    return pltpu.make_async_copy(src.at[at], dst.at[at], sem.at[k])


def analyse_body(v, depth, middle, out, have, first, work, sem):
    for k in range(8):
        chunk_copy(v, have, sem, k).start()
    table = owner_table(depth)
    for k in range(8):
        chunk_copy(v, have, sem, k).wait()
        analyse_rows(have[k * 512 : k * 512 + 512, :], k, table, first)
    by_owner(first, middle, out, work)


def whole(shape):
    return pl.BlockSpec(shape, lambda i: (0,) * len(shape))


HBM = pl.BlockSpec(memory_space=pl.ANY)
VM = pl.BlockSpec(memory_space=pltpu.VMEM)
GRID_ROWS = jax.ShapeDtypeStruct((4096, ZT), BF)
SENT = jax.ShapeDtypeStruct((ND, 48, 128), BF)


def analyse(values, t):
    return pl.pallas_call(
        analyse_body,
        in_specs=[HBM, VM, VM],
        out_specs=VM,
        out_shape=SENT,
        scratch_shapes=[
            pltpu.VMEM((4096, ZT), BF), pltpu.VMEM((768, 1024), BF),
            pltpu.VMEM((NQ, 512, 128), F32), pltpu.SemaphoreType.DMA((8,)),
        ],
        name="analyse",
    )(values, t["depth"], t["middle"])


def spectrum_rows(got, ana_out, perm, scale):
    parts = dot(ana_out[...], got[...].reshape(512, 128))
    if scale is not None:
        parts = parts * scale
    parts = parts.astype(BF)
    joined = jnp.concatenate([parts[g * 32 : g * 32 + 32] for g in range(4)], axis=1)
    return dot(joined, perm[...])


def mode_mask():
    lane = lax.broadcasted_iota(jnp.int32, (8, 256), 1) // 32
    return lane == lax.broadcasted_iota(jnp.int32, (8, 256), 0)


def scatter_owner(synth, work, out):
    for r in range(2):
        for xi in range(2):
            for g in range(4):
                at = (r * 2 + xi) * 32
                work[pl.ds(r * 8 + xi * 4 + g, ND, stride=16), :] = synth[
                    at : at + 32, g * 128 : g * 128 + 128
                ]
    out[...] = work[...].reshape(ND, 16, 128).astype(BF)


def mix_forward_body(got, w, ana_out, perm, spread, fwd_out, out, spec, srow, mixed, work):
    rows = spectrum_rows(got, ana_out, perm, None)
    spec[...] = rows.astype(BF)
    srow[...] = rows
    mask = mode_mask()
    for kx in range(MX):
        for h in range(2):
            lanes = slice(h * 256, h * 256 + 256)
            real = jnp.where(mask, jnp.broadcast_to(srow[kx : kx + 1, lanes], (8, 256)), 0.0)
            imag = jnp.where(mask, jnp.broadcast_to(srow[16 + kx : 17 + kx, lanes], (8, 256)), 0.0)
            left = jnp.concatenate([real, imag], axis=0).astype(BF)
            at = (kx * 2 + h) * 256
            both = dot(left, w[at : at + 256, :])
            low = both[8:16]
            turned = jnp.concatenate([-low[:, 32:], low[:, :32]], axis=1)
            mixed[kx * 16 + h * 8 : kx * 16 + h * 8 + 8, :] = both[:8] + turned
    values = mixed[...].astype(BF)
    row_ky = lax.broadcasted_iota(jnp.int32, (256, 512), 0) % 16
    lane_ky = lax.broadcasted_iota(jnp.int32, (256, 512), 1) // 8 % 16
    same = row_ky == lane_ky
    wide = [jnp.where(same, dot(values, spread[p]), 0.0).astype(BF) for p in range(2)]
    synth = dot(fwd_out[...], jnp.concatenate(wide, axis=0))
    scatter_owner(synth, work, out)


def squeezed(shape):
    return pl.BlockSpec((None,) + shape, lambda i: (i,) + (0,) * len(shape))


def slot_spec():
    return pl.BlockSpec((ND, 16, 128), lambda i: (0, i, 0))


def mix_forward(got, weights, t):
    return pl.pallas_call(
        mix_forward_body,
        grid=(NQ,),
        in_specs=[
            slot_spec(), squeezed((8192, 64)), whole((128, 512)), whole((512, 512)),
            whole((2, 64, 512)), whole((128, 512)),
        ],
        out_specs=[slot_spec(), squeezed((32, 512))],
        out_shape=[
            jax.ShapeDtypeStruct((ND, 48, 128), BF),
            jax.ShapeDtypeStruct((NQ, 32, 512), BF),
        ],
        scratch_shapes=[
            pltpu.VMEM((32, 512), F32), pltpu.VMEM((256, 64), F32), pltpu.VMEM((512, 128), F32),
        ],
        name="mix_forward",
    )(got, weights, t["ana_out"], t["perm"], t["spread"], t["fwd_out"])


def mix_backward_body(
    got, w, ana_out, perm, fold, bwd_out, out, spec, srow, pair, masked, work
):
    rows = spectrum_rows(got, ana_out, perm, SCALE)
    spec[...] = rows.astype(BF)
    srow[...] = rows
    mask = mode_mask()
    for h in range(2):
        total = None
        for part in range(2):
            lanes = slice(h * 256, h * 256 + 256)
            tall = [
                jnp.where(mask, jnp.broadcast_to(srow[k : k + 1, lanes], (8, 256)), 0.0)
                for k in range(part * 16, part * 16 + 16)
            ]
            one = dot(jnp.concatenate(tall, axis=0).astype(BF), fold[part])
            total = one if total is None else total + one
        pair[h] = total
    for kx in range(MX):
        for h in range(2):
            both = pair[h, kx * 8 : kx * 8 + 8, :]
            left = jnp.concatenate([both[:, :64], both[:, 64:]], axis=0).astype(BF)
            at = (kx * 2 + h) * 256
            full = dot_t(left, w[at : at + 256, :])
            masked[h, kx * 8 : kx * 8 + 8, :] = jnp.where(mask, full[:8], 0.0)
            masked[h, 128 + kx * 8 : 136 + kx * 8, :] = jnp.where(mask, full[8:], 0.0)
    synth = [dot(bwd_out[...], masked[h].astype(BF)).astype(BF) for h in range(2)]
    turned = dot_t(jnp.concatenate(synth, axis=1), perm[...])
    scatter_owner(turned, work, out)


def mix_backward(got, weights, t):
    return pl.pallas_call(
        mix_backward_body,
        grid=(NQ,),
        in_specs=[
            slot_spec(), squeezed((8192, 64)), whole((128, 512)), whole((512, 512)),
            whole((2, 256, 128)), whole((128, 256)),
        ],
        out_specs=[slot_spec(), squeezed((32, 512))],
        out_shape=[
            jax.ShapeDtypeStruct((ND, 48, 128), BF),
            jax.ShapeDtypeStruct((NQ, 32, 512), BF),
        ],
        scratch_shapes=[
            pltpu.VMEM((32, 512), F32), pltpu.VMEM((2, 128, 128), F32),
            pltpu.VMEM((2, 256, 256), F32), pltpu.VMEM((512, 128), F32),
        ],
        name="mix_backward",
    )(got, weights, t["ana_out"], t["perm"], t["fold"], t["bwd_out"])


def unpack(got, have, turned, middle, tall):
    for qi in range(NQ):
        have[qi] = got[:, qi * 16 : qi * 16 + 16, :].reshape(512, 128).astype(F32)
    for slot in range(8):
        for p in range(2):
            pieces = [have[qi, pl.ds(p * 8 + slot, ND, stride=16), :] for qi in range(NQ)]
            pieces.append(jnp.zeros((ND, 128), F32))
            turned[slot * 128 : slot * 128 + 128, p * 128 : p * 128 + 128] = jnp.concatenate(
                pieces, axis=0
            ).astype(BF)
    for r in range(2):
        block = dot_t(middle[r * 512 : r * 512 + 512, :], turned[...]).astype(BF)
        for slot in range(8):
            tall[slot * 512 : slot * 512 + 512, r * 128 : r * 128 + 128] = block[
                :, slot * 128 : slot * 128 + 128
            ]


ROOT = math.sqrt(2.0 / math.pi)
CHUNK = 128


def activate_body(
    got, lin, cot, depth, middle, act, grad, out, lin_v, cot_v, act_v, grad_v, have, turned, tall,
    first, work, sems,
):
    for k in range(8):
        chunk_copy(lin, lin_v, sems.at[0], k).start()
        chunk_copy(cot, cot_v, sems.at[1], k).start()
    unpack(got, have, turned, middle, tall)

    def step(k, carry):
        chunk_copy(lin, lin_v, sems.at[0], k).wait()
        chunk_copy(cot, cot_v, sems.at[1], k).wait()
        for j in range(512 // CHUNK):
            at = pl.ds(pl.multiple_of(k * 512 + j * CHUNK, CHUNK), CHUNK)
            v = dot(tall[at, :], depth[...]) + lin_v[at, :].astype(F32)
            square = v * v
            half = 0.5 + 0.5 * jnp.tanh(v * (ROOT + (ROOT * 0.044715) * square))
            value = v * half
            slope = half + (value - value * half) * (2.0 * ROOT + (6.0 * ROOT * 0.044715) * square)
            act_v[at, :] = value.astype(BF)
            grad_v[at, :] = (cot_v[at, :].astype(F32) * slope).astype(BF)
        chunk_copy(act_v, act, sems.at[2], k).start()
        chunk_copy(grad_v, grad, sems.at[3], k).start()
        rows = grad_v[pl.ds(pl.multiple_of(k * 512, 512), 512), :]
        analyse_rows(rows, k, owner_table(depth), first)
        return carry

    lax.fori_loop(0, 8, step, 0)
    by_owner(first, middle, out, work)
    for k in range(8):
        chunk_copy(act_v, act, sems.at[2], k).wait()
        chunk_copy(grad_v, grad, sems.at[3], k).wait()


SYNTH_SCRATCH = [
    pltpu.VMEM((NQ, 512, 128), F32), pltpu.VMEM((1024, 256), BF), pltpu.VMEM((4096, 256), BF),
]


def activate(got, lin, cot, t):
    return pl.pallas_call(
        activate_body,
        in_specs=[VM, HBM, HBM, VM, VM],
        out_specs=[HBM, HBM, VM],
        out_shape=[GRID_ROWS, GRID_ROWS, SENT],
        scratch_shapes=[pltpu.VMEM((4096, ZT), BF)] * 4
        + SYNTH_SCRATCH
        + [
            pltpu.VMEM((768, 1024), BF), pltpu.VMEM((NQ, 512, 128), F32),
            pltpu.SemaphoreType.DMA((4, 8)),
        ],
        name="activate",
    )(got, lin, cot, t["depth"], t["middle"])


def finish_body(got, lin, depth, middle, out, lin_v, out_v, have, turned, tall, sems):
    for k in range(8):
        chunk_copy(lin, lin_v, sems.at[0], k).start()
    unpack(got, have, turned, middle, tall)

    def step(k, carry):
        chunk_copy(lin, lin_v, sems.at[0], k).wait()
        at = pl.ds(pl.multiple_of(k * 512, 512), 512)
        out_v[at, :] = (dot(tall[at, :], depth[...]) + lin_v[at, :].astype(F32)).astype(BF)
        chunk_copy(out_v, out, sems.at[1], k).start()
        return carry

    lax.fori_loop(0, 8, step, 0)
    for k in range(8):
        chunk_copy(out_v, out, sems.at[1], k).wait()


def finish(got, lin, t):
    return pl.pallas_call(
        finish_body,
        in_specs=[VM, HBM, VM, VM],
        out_specs=HBM,
        out_shape=GRID_ROWS,
        scratch_shapes=[pltpu.VMEM((4096, ZT), BF)] * 2
        + SYNTH_SCRATCH
        + [pltpu.SemaphoreType.DMA((2, 8))],
        name="finish",
    )(got, lin, t["depth"], t["middle"])


def linear_body(turn, v, matrix, bias, out, have, made, kron, sems):
    for k in range(8):
        chunk_copy(v, have, sems.at[0], k).start()
    rows = lax.broadcasted_iota(jnp.int32, (512, C), 0) // 16
    pick = jnp.where(rows == lax.broadcasted_iota(jnp.int32, (512, C), 1), 1.0, 0.0).astype(BF)
    if turn:
        wide = lax.dot_general(matrix[...], pick, (((0,), (1,)), ((), ())), preferred_element_type=F32)
    else:
        wide = dot_t(matrix[...], pick)
    tall = dot(pick, wide.astype(BF))
    row = lax.broadcasted_iota(jnp.int32, (512, 512), 0) % 16
    col = lax.broadcasted_iota(jnp.int32, (512, 512), 1) % 16
    kron[...] = jnp.where(row == col, tall, 0.0).astype(BF)
    for x in range(2):
        for k in range(4):
            chunk_copy(v, have, sems.at[0], x * 4 + k).wait()
        grid = have.at[pl.ds(x * 2048, 2048)].reshape(C, Y, ZT)
        done = made.at[pl.ds(x * 2048, 2048)].reshape(C, Y, ZT)
        for g in range(4):
            cells = grid[:, g * 16 : g * 16 + 16, :].reshape(512, ZT)
            result = dot(kron[...], cells)
            for c in range(C):
                one = result[c * 16 : c * 16 + 16]
                if bias is not None:
                    one = one + bias[c]
                done[c, g * 16 : g * 16 + 16, :] = one.astype(BF)
        for k in range(4):
            chunk_copy(made, out, sems.at[1], x * 4 + k).start()
    for k in range(8):
        chunk_copy(made, out, sems.at[1], k).wait()


def linear(values, matrix, bias, turn):
    if bias is None:
        body = lambda v, m, *rest: linear_body(turn, v, m, None, *rest)
        more = []
    else:
        body = partial(linear_body, turn)
        more = [bias]
    return pl.pallas_call(
        body,
        in_specs=[HBM, VM] + [pl.BlockSpec(memory_space=pltpu.SMEM)] * len(more),
        out_specs=HBM,
        out_shape=GRID_ROWS,
        scratch_shapes=[
            pltpu.VMEM((4096, ZT), BF), pltpu.VMEM((4096, ZT), BF), pltpu.VMEM((512, 512), BF),
            pltpu.SemaphoreType.DMA((2, 8)),
        ],
        name="linear",
    )(values, matrix, *more)


def weight_body(*refs):
    specs, grads = refs[:4], refs[4:8]
    fold, out, srow, grow, made, sem = refs[8:]
    for s in range(4):
        srow[s] = specs[s][...].astype(F32)
        grow[s] = grads[s][...].astype(F32)

    mask = mode_mask()
    low = lax.broadcasted_iota(jnp.int32, (32, 128), 1) < 64
    blank = jnp.zeros((64, 128), F32)

    def tall(ref, qi, group, s, p, j, h):
        row = ref[s, qi, pl.ds(p * 16 + group * 4 + j, 1), h * 256 : h * 256 + 256]
        return jnp.where(mask, jnp.broadcast_to(row, (8, 256)), 0.0)

    def copy_out(i):
        at = pl.ds(pl.multiple_of(i * 2048, 2048), 2048)
        return pltpu.make_async_copy(made.at[at], out.at[at], sem.at[i])

    def step(i, carry):
        qi, group = i // 4, i % 4
        for h in range(2):
            left = [
                tall(srow, qi, group, s, p, j, h) for j in range(4) for p in range(2) for s in range(4)
            ]
            left = jnp.concatenate(left, axis=0).astype(BF)
            pair = None
            for p in range(2):
                rows = [tall(grow, qi, group, s, p, j, h) for j in range(4) for s in range(4)]
                one = dot(jnp.concatenate(rows, axis=0).astype(BF), fold[p])
                pair = one if pair is None else pair + one
            blocks = []
            for j in range(4):
                here = pair[j * 32 : j * 32 + 32]
                there = jnp.concatenate([here[:, 64:], here[:, :64]], axis=1)
                if j % 2 == 0:
                    one, two = jnp.where(low, here, 0.0), jnp.where(low, there, 0.0)
                else:
                    one, two = jnp.where(low, 0.0, there), jnp.where(low, 0.0, here)
                piece = jnp.concatenate([one, two], axis=0)
                blocks.append(jnp.concatenate([piece, blank] if j < 2 else [blank, piece], axis=1))
            right = jnp.concatenate(blocks, axis=0).astype(BF)
            grad = lax.dot_general(left, right, (((0,), (0,)), ((), ())), preferred_element_type=F32)
            for j in range(4):
                at = pl.ds(pl.multiple_of(i * 2048 + (j * 2 + h) * 256, 256), 256)
                made[at, :] = grad[:, j * 64 : j * 64 + 64]
        copy_out(i).start()
        return carry

    lax.fori_loop(0, NQ * 4, step, 0)
    for i in range(NQ * 4):
        copy_out(i).wait()


def weight_gradient(specs, grads, t):
    return pl.pallas_call(
        weight_body,
        in_specs=[VM] * 9,
        out_specs=HBM,
        out_shape=jax.ShapeDtypeStruct((NQ * 8192, 64), F32),
        scratch_shapes=[pltpu.VMEM((4, NQ, 32, 512), F32), pltpu.VMEM((4, NQ, 32, 512), F32)]
        + [pltpu.VMEM((NQ * 8192, 64), F32), pltpu.SemaphoreType.DMA((NQ * 4,))],
        name="weight_gradient",
    )(*specs, *grads, t["fold"])


def exchange(values):
    return lax.all_to_all(values, "slab", split_axis=0, concat_axis=0, tiled=True)


def everyone(values):
    pieces = [values]
    for k in range(1, 4):
        pieces.append(lax.ppermute(values, "dp", [(i, i ^ k) for i in range(4)]))
    return pieces


def per_device(field, cotangent, spectral_weight, point_weight, bias_term):
    t = tables()
    rows = field.reshape(4096, ZT)
    weights = spectral_weight.reshape(NQ, 8192, 64)
    sent = exchange(analyse(rows, t))
    lin = linear(rows, point_weight, bias_term, False)
    sent, lin = lax.optimization_barrier((sent, lin))
    back, spec = mix_forward(sent, weights, t)
    got = exchange(back)
    specs = everyone(spec)
    act, grad_pre, out = activate(got, lin, cotangent.reshape(4096, ZT), t)
    sent = exchange(out)
    lin = linear(grad_pre, point_weight, None, True)
    sent, lin = lax.optimization_barrier((sent, lin))
    back, grad_spec = mix_backward(sent, weights, t)
    got = exchange(back)
    grads = everyone(grad_spec)
    weight_grad = weight_gradient(specs, grads, t).reshape(NQ, MX, MY, C, 2 * C)
    got, weight_grad = lax.optimization_barrier((got, weight_grad))
    total = finish(got, lin, t)
    shape = (1, 2, C, Y, ZT)
    return act.reshape(shape), total.reshape(shape), weight_grad


def solution(mesh):
    placed = (
        P("dp", "slab", None, None, None),
        P("dp", "slab", None, None, None),
        P("slab", None, None, None, None),
        P(),
        P(),
    )
    return jax.shard_map(
        per_device,
        mesh=mesh,
        in_specs=placed,
        out_specs=(
            P("dp", "slab", None, None, None),
            P("dp", "slab", None, None, None),
            P("slab", None, None, None, None),
        ),
        check_vma=False,
    )
```

```python
import math
from functools import partial

import jax
import jax.numpy as jnp
import numpy as np
from jax import lax
from jax.experimental import pallas as pl
from jax.experimental.pallas import tpu as pltpu
from jax.sharding import PartitionSpec as P

X = 64
Y = 64
Z = 32
T_SIZE = 16
ZT = Z * T_SIZE
C = 32
MX = 16
MY = 16
MZ = 12
MT = 8
NQ = 3
ND = 32
SCALE = 1.0 / (X * Y * Z * T_SIZE)
BF = jnp.bfloat16
F32 = jnp.float32


def signed(modes):
    i = np.arange(modes)
    return np.where(i < modes // 2, i, i - modes)


def inner_np():
    q = np.arange(MZ * MT)
    place = np.arange(ZT)
    kz = (signed(MZ)[q // MT] % Z)[:, None]
    kt = (q % MT)[:, None]
    counts = kz * (place // T_SIZE)[None] % Z * T_SIZE + kt * (place % T_SIZE)[None] % T_SIZE * Z
    angle = 2.0 * math.pi / ZT * (counts % ZT)
    return np.stack([np.cos(angle), -np.sin(angle)]).astype(np.float32)


def complex_np(modes, length):
    k = (signed(modes) % length)[:, None]
    angle = 2.0 * math.pi / length * (k * np.arange(length)[None] % length)
    c, s = np.cos(angle), np.sin(angle)
    return np.stack([np.stack([c, s], 1), np.stack([-s, c], 1)]).astype(np.float32)


def tables():
    inner = inner_np()
    mid = complex_np(MY, Y)
    out = complex_np(MX, X)
    depth = np.zeros((2, 128, ZT), np.float32)
    depth[:, :96] = inner.reshape(2, ND, NQ, ZT).transpose(0, 2, 1, 3).reshape(2, 96, ZT)
    depth = depth.reshape(256, ZT)
    middle = np.einsum("rkpy,cd->pcyrkd", mid, np.eye(8, dtype=np.float32)).reshape(1024, 256)
    eye4 = np.eye(4, dtype=np.float32)
    ana_out = np.einsum("rkpsi,gh->grkspih", out.reshape(2, MX, 2, ND, 2), eye4).reshape(128, 512)
    syn_out = out.reshape(2, MX, 2, ND, 2).transpose(2, 4, 3, 0, 1)
    fwd_out = np.repeat(syn_out.reshape(128, 32), 16, axis=1)
    bwd_out = np.repeat(syn_out.reshape(128, 32), 8, axis=1)
    spread = np.zeros((2, 2, 4, 8, 4, MY, 8), np.float32)
    for g in range(4):
        for c in range(8):
            spread[0, 0, g, c, g, :, c] = 1.0
            spread[1, 1, g, c, g, :, c] = 1.0
    spread = spread.reshape(2, 64, 512)
    fold = np.zeros((2, 8, C, 128), np.float32)
    for o in range(C):
        fold[0, :, o, o] = 1.0
        fold[0, :, o, 96 + o] = -1.0
        fold[1, :, o, 32 + o] = 1.0
        fold[1, :, o, 64 + o] = 1.0
    fold = fold.reshape(512, 128)
    t = dict(
        depth=depth, middle=middle, ana_out=ana_out, fwd_out=fwd_out * SCALE, bwd_out=bwd_out,
        spread=spread, fold=fold,
    )
    return {k: jnp.asarray(v, BF) for k, v in t.items()}


def dot(a, b):
    return lax.dot_general(a, b, (((1,), (0,)), ((), ())), preferred_element_type=F32)


def dot_t(a, b):
    return lax.dot_general(a, b, (((1,), (1,)), ((), ())), preferred_element_type=F32)


def owner_table(depth):
    return jnp.concatenate([depth[0:96, :], depth[128:224, :]], axis=0)


def analyse_rows(rows, slot, table, first):
    part = dot_t(table, rows).astype(BF)
    at = pl.ds(slot * 96, 96) if isinstance(slot, int) else pl.ds(pl.multiple_of(slot * 96, 32), 96)
    first[at, 0:512] = part[:96]
    first[at, 512:1024] = part[96:]


def by_owner(first, middle, out, work):
    second = dot(first[...], middle[...])
    for slot in range(8):
        for qi in range(NQ):
            for r in range(2):
                at = slot * 96 + qi * 32
                work[qi, pl.ds(r * 8 + slot, ND, stride=16), :] = second[
                    at : at + 32, r * 128 : r * 128 + 128
                ]
    for qi in range(NQ):
        out[:, qi * 16 : qi * 16 + 16, :] = work[qi].reshape(ND, 16, 128).astype(BF)


def chunk_copy(src, dst, sem, k):
    at = pl.ds(k * 512, 512)
    return pltpu.make_async_copy(src.at[at], dst.at[at], sem.at[k])


def analyse_body(v, depth, middle, out, have, first, work, sem):
    for k in range(8):
        chunk_copy(v, have, sem, k).start()
    table = owner_table(depth)
    for k in range(8):
        chunk_copy(v, have, sem, k).wait()
        analyse_rows(have[k * 512 : k * 512 + 512, :], k, table, first)
    by_owner(first, middle, out, work)


def whole(shape):
    return pl.BlockSpec(shape, lambda i: (0,) * len(shape))


HBM = pl.BlockSpec(memory_space=pltpu.HBM)
VM = pl.BlockSpec(memory_space=pltpu.VMEM)
GRID_ROWS = jax.ShapeDtypeStruct((4096, ZT), BF)
SENT = jax.ShapeDtypeStruct((ND, 48, 128), BF)


def analyse(values, t):
    return pl.pallas_call(
        analyse_body,
        in_specs=[HBM, VM, VM],
        out_specs=VM,
        out_shape=SENT,
        scratch_shapes=[
            pltpu.VMEM((4096, ZT), BF), pltpu.VMEM((768, 1024), BF),
            pltpu.VMEM((NQ, 512, 128), F32), pltpu.SemaphoreType.DMA((8,)),
        ],
        name="analyse",
        compiler_params=pltpu.CompilerParams(vmem_limit_bytes=52 << 20),
    )(values, t["depth"], t["middle"])


def channel_order(perm):
    row = lax.broadcasted_iota(jnp.int32, (512, 512), 0)
    col = lax.broadcasted_iota(jnp.int32, (512, 512), 1)
    place = row // 8 % 16 * 32 + row // 128 * 8 + row % 8
    perm[...] = jnp.where(place == col, 1.0, 0.0).astype(BF)


def spectrum_rows(got, ana_out, perm, scale):
    tall = [got[:, q * 16 : q * 16 + 16, :].reshape(512, 128) for q in range(NQ)]
    parts = dot(ana_out[...], jnp.concatenate(tall, axis=1))
    if scale is not None:
        parts = parts * scale
    parts = parts.astype(BF)
    rows = [
        jnp.concatenate([parts[g * 32 : g * 32 + 32, q * 128 : q * 128 + 128] for g in range(4)], axis=1)
        for q in range(NQ)
    ]
    return dot(jnp.concatenate(rows, axis=0), perm[...])


def mode_mask():
    lane = lax.broadcasted_iota(jnp.int32, (8, 256), 1) // 32
    return lane == lax.broadcasted_iota(jnp.int32, (8, 256), 0)


def scatter_owner(synth, q, work, out):
    for r in range(2):
        for xi in range(2):
            for g in range(4):
                at = (r * 2 + xi) * 32
                work[q, pl.ds(r * 8 + xi * 4 + g, ND, stride=16), :] = synth[
                    at : at + 32, g * 128 : g * 128 + 128
                ]
    out[:, q * 16 : q * 16 + 16, :] = work[q].reshape(ND, 16, 128).astype(BF)


def weight_copy(w, have, sem, q):
    return pltpu.make_async_copy(w.at[q], have.at[q], sem.at[q])


def mix_forward_body(
    got, w, ana_out, spread, fwd_out, out, spec, have, srow, mixed, work, perm, sem
):
    for q in range(NQ):
        weight_copy(w, have, sem, q).start()
    channel_order(perm)
    rows = spectrum_rows(got, ana_out, perm, None)
    srow[...] = rows
    for q in range(NQ):
        spec[q] = rows[q * 32 : q * 32 + 32].astype(BF)
    mask = mode_mask()
    row_ky = lax.broadcasted_iota(jnp.int32, (256, 512), 0) % 16
    lane_ky = lax.broadcasted_iota(jnp.int32, (256, 512), 1) // 8 % 16
    same = row_ky == lane_ky
    for q in range(NQ):
        weight_copy(w, have, sem, q).wait()
        for kx in range(MX):
            for h in range(2):
                lanes = slice(h * 256, h * 256 + 256)
                at = q * 32 + kx
                real = jnp.where(mask, jnp.broadcast_to(srow[at : at + 1, lanes], (8, 256)), 0.0)
                at = at + 16
                imag = jnp.where(mask, jnp.broadcast_to(srow[at : at + 1, lanes], (8, 256)), 0.0)
                left = jnp.concatenate([real, imag], axis=0).astype(BF)
                at = (kx * 2 + h) * 256
                both = dot(left, have[q, at : at + 256, :])
                low = both[8:16]
                turned = jnp.concatenate([-low[:, 32:], low[:, :32]], axis=1)
                at = kx * 16 + h * 8
                mixed[q, at : at + 8, :] = both[:8] + turned
        values = mixed[q].astype(BF)
        wide = [jnp.where(same, dot(values, spread[p]), 0.0).astype(BF) for p in range(2)]
        synth = dot(fwd_out[...], jnp.concatenate(wide, axis=0))
        scatter_owner(synth, q, work, out)


SPECTRUM = jax.ShapeDtypeStruct((NQ, 32, 512), BF)


def mix_forward(got, weights, t):
    return pl.pallas_call(
        mix_forward_body,
        in_specs=[VM, HBM, VM, VM, VM],
        out_specs=[VM, VM],
        out_shape=[SENT, SPECTRUM],
        scratch_shapes=[
            pltpu.VMEM((NQ, 8192, 64), BF), pltpu.VMEM((96, 512), F32), pltpu.VMEM((NQ, 256, 64), F32),
            pltpu.VMEM((NQ, 512, 128), F32), pltpu.VMEM((512, 512), BF),
            pltpu.SemaphoreType.DMA((NQ,)),
        ],
        name="mix_forward",
        compiler_params=pltpu.CompilerParams(vmem_limit_bytes=52 << 20),
    )(got, weights, t["ana_out"], t["spread"], t["fwd_out"])


def mix_backward_body(
    got, w, ana_out, fold, bwd_out, out, spec, have, srow, pair, masked, work, perm, sem
):
    for q in range(NQ):
        weight_copy(w, have, sem, q).start()
    channel_order(perm)
    rows = spectrum_rows(got, ana_out, perm, SCALE)
    srow[...] = rows
    for q in range(NQ):
        spec[q] = rows[q * 32 : q * 32 + 32].astype(BF)
    mask = mode_mask()
    for h in range(2):
        lanes = slice(h * 256, h * 256 + 256)
        sides = []
        for part in range(2):
            tall = [
                jnp.where(mask, jnp.broadcast_to(srow[k : k + 1, lanes], (8, 256)), 0.0)
                for q in range(NQ)
                for k in range(q * 32 + part * 16, q * 32 + part * 16 + 16)
            ]
            sides.append(jnp.concatenate(tall, axis=0).astype(BF))
        pair[h] = dot(jnp.concatenate(sides, axis=1), fold[...])
    for q in range(NQ):
        weight_copy(w, have, sem, q).wait()
        for kx in range(MX):
            for h in range(2):
                at = q * 128 + kx * 8
                both = pair[h, at : at + 8, :]
                left = jnp.concatenate([both[:, :64], both[:, 64:]], axis=0).astype(BF)
                at = (kx * 2 + h) * 256
                full = dot_t(left, have[q, at : at + 256, :])
                masked[q, h, kx * 8 : kx * 8 + 8, :] = jnp.where(mask, full[:8], 0.0)
                masked[q, h, 128 + kx * 8 : 136 + kx * 8, :] = jnp.where(mask, full[8:], 0.0)
        synth = [dot(bwd_out[...], masked[q, h].astype(BF)).astype(BF) for h in range(2)]
        turned = dot_t(jnp.concatenate(synth, axis=1), perm[...])
        scatter_owner(turned, q, work, out)


def mix_backward(got, weights, t):
    return pl.pallas_call(
        mix_backward_body,
        in_specs=[VM, HBM, VM, VM, VM],
        out_specs=[VM, VM],
        out_shape=[SENT, SPECTRUM],
        scratch_shapes=[
            pltpu.VMEM((NQ, 8192, 64), BF), pltpu.VMEM((96, 512), F32), pltpu.VMEM((2, 384, 128), F32),
            pltpu.VMEM((NQ, 2, 256, 256), F32), pltpu.VMEM((NQ, 512, 128), F32),
            pltpu.VMEM((512, 512), BF), pltpu.SemaphoreType.DMA((NQ,)),
        ],
        name="mix_backward",
        compiler_params=pltpu.CompilerParams(vmem_limit_bytes=52 << 20),
    )(got, weights, t["ana_out"], t["fold"], t["bwd_out"])


def unpack(got, have, turned, middle, tall):
    for qi in range(NQ):
        have[qi] = got[:, qi * 16 : qi * 16 + 16, :].reshape(512, 128).astype(F32)
    for slot in range(8):
        for p in range(2):
            pieces = [have[qi, pl.ds(p * 8 + slot, ND, stride=16), :] for qi in range(NQ)]
            pieces.append(jnp.zeros((ND, 128), F32))
            turned[slot * 128 : slot * 128 + 128, p * 128 : p * 128 + 128] = jnp.concatenate(
                pieces, axis=0
            ).astype(BF)
    for r in range(2):
        block = dot_t(middle[r * 512 : r * 512 + 512, :], turned[...]).astype(BF)
        for slot in range(8):
            tall[slot * 512 : slot * 512 + 512, r * 128 : r * 128 + 128] = block[
                :, slot * 128 : slot * 128 + 128
            ]


ROOT = math.sqrt(2.0 / math.pi)
CHUNK = 512


def activate_body(
    got, lin, cot, depth, middle, act, grad, out, lin_v, cot_v, act_v, grad_v, have, turned, tall,
    first, work, sems,
):
    for k in range(8):
        chunk_copy(lin, lin_v, sems.at[0], k).start()
        chunk_copy(cot, cot_v, sems.at[1], k).start()
    unpack(got, have, turned, middle, tall)

    def step(k, carry):
        chunk_copy(lin, lin_v, sems.at[0], k).wait()
        chunk_copy(cot, cot_v, sems.at[1], k).wait()
        for j in range(512 // CHUNK):
            at = pl.ds(pl.multiple_of(k * 512 + j * CHUNK, CHUNK), CHUNK)
            v = dot(tall[at, :], depth[...]) + lin_v[at, :].astype(F32)
            square = v * v
            half = 0.5 + 0.5 * jnp.tanh(v * (ROOT + (ROOT * 0.044715) * square))
            value = v * half
            slope = half + (value - value * half) * (2.0 * ROOT + (6.0 * ROOT * 0.044715) * square)
            act_v[at, :] = value.astype(BF)
            grad_v[at, :] = (cot_v[at, :].astype(F32) * slope).astype(BF)
        chunk_copy(act_v, act, sems.at[2], k).start()
        chunk_copy(grad_v, grad, sems.at[3], k).start()
        rows = grad_v[pl.ds(pl.multiple_of(k * 512, 512), 512), :]
        analyse_rows(rows, k, owner_table(depth), first)
        return carry

    lax.fori_loop(0, 8, step, 0)
    by_owner(first, middle, out, work)
    for k in range(8):
        chunk_copy(act_v, act, sems.at[2], k).wait()
        chunk_copy(grad_v, grad, sems.at[3], k).wait()


SYNTH_SCRATCH = [
    pltpu.VMEM((NQ, 512, 128), F32), pltpu.VMEM((1024, 256), BF), pltpu.VMEM((4096, 256), BF),
]


def activate(got, lin, cot, t):
    return pl.pallas_call(
        activate_body,
        in_specs=[VM, HBM, HBM, VM, VM],
        out_specs=[HBM, HBM, VM],
        out_shape=[GRID_ROWS, GRID_ROWS, SENT],
        scratch_shapes=[pltpu.VMEM((4096, ZT), BF)] * 4
        + SYNTH_SCRATCH
        + [
            pltpu.VMEM((768, 1024), BF), pltpu.VMEM((NQ, 512, 128), F32),
            pltpu.SemaphoreType.DMA((4, 8)),
        ],
        name="activate",
        compiler_params=pltpu.CompilerParams(vmem_limit_bytes=52 << 20),
    )(got, lin, cot, t["depth"], t["middle"])


def finish_body(got, lin, depth, middle, out, lin_v, out_v, have, turned, tall, sems):
    for k in range(8):
        chunk_copy(lin, lin_v, sems.at[0], k).start()
    unpack(got, have, turned, middle, tall)

    def step(k, carry):
        chunk_copy(lin, lin_v, sems.at[0], k).wait()
        at = pl.ds(pl.multiple_of(k * 512, 512), 512)
        out_v[at, :] = (dot(tall[at, :], depth[...]) + lin_v[at, :].astype(F32)).astype(BF)
        chunk_copy(out_v, out, sems.at[1], k).start()
        return carry

    lax.fori_loop(0, 8, step, 0)
    for k in range(8):
        chunk_copy(out_v, out, sems.at[1], k).wait()


def finish(got, lin, t):
    return pl.pallas_call(
        finish_body,
        in_specs=[VM, HBM, VM, VM],
        out_specs=HBM,
        out_shape=GRID_ROWS,
        scratch_shapes=[pltpu.VMEM((4096, ZT), BF)] * 2
        + SYNTH_SCRATCH
        + [pltpu.SemaphoreType.DMA((2, 8))],
        name="finish",
        compiler_params=pltpu.CompilerParams(vmem_limit_bytes=52 << 20),
    )(got, lin, t["depth"], t["middle"])


def linear_body(turn, v, matrix, bias, out, have, made, kron, sems):
    for k in range(8):
        chunk_copy(v, have, sems.at[0], k).start()
    rows = lax.broadcasted_iota(jnp.int32, (512, C), 0) // 16
    pick = jnp.where(rows == lax.broadcasted_iota(jnp.int32, (512, C), 1), 1.0, 0.0).astype(BF)
    if turn:
        wide = lax.dot_general(matrix[...], pick, (((0,), (1,)), ((), ())), preferred_element_type=F32)
    else:
        wide = dot_t(matrix[...], pick)
    tall = dot(pick, wide.astype(BF))
    row = lax.broadcasted_iota(jnp.int32, (512, 512), 0) % 16
    col = lax.broadcasted_iota(jnp.int32, (512, 512), 1) % 16
    kron[...] = jnp.where(row == col, tall, 0.0).astype(BF)
    for x in range(2):
        for k in range(4):
            chunk_copy(v, have, sems.at[0], x * 4 + k).wait()
        grid = have.at[pl.ds(x * 2048, 2048)].reshape(C, Y, ZT)
        done = made.at[pl.ds(x * 2048, 2048)].reshape(C, Y, ZT)
        for g in range(4):
            cells = grid[:, g * 16 : g * 16 + 16, :].reshape(512, ZT)
            result = dot(kron[...], cells)
            for c in range(C):
                one = result[c * 16 : c * 16 + 16]
                if bias is not None:
                    one = one + bias[c]
                done[c, g * 16 : g * 16 + 16, :] = one.astype(BF)
        for k in range(4):
            chunk_copy(made, out, sems.at[1], x * 4 + k).start()
    for k in range(8):
        chunk_copy(made, out, sems.at[1], k).wait()


def linear(values, matrix, bias, turn):
    if bias is None:
        body = lambda v, m, *rest: linear_body(turn, v, m, None, *rest)
        more = []
    else:
        body = partial(linear_body, turn)
        more = [bias]
    return pl.pallas_call(
        body,
        in_specs=[HBM, VM] + [pl.BlockSpec(memory_space=pltpu.SMEM)] * len(more),
        out_specs=HBM,
        out_shape=GRID_ROWS,
        scratch_shapes=[
            pltpu.VMEM((4096, ZT), BF), pltpu.VMEM((4096, ZT), BF), pltpu.VMEM((512, 512), BF),
            pltpu.SemaphoreType.DMA((2, 8)),
        ],
        name="linear",
        compiler_params=pltpu.CompilerParams(vmem_limit_bytes=52 << 20),
    )(values, matrix, *more)


def weight_body(*refs):
    specs, grads = refs[:2], refs[2:4]
    fold, out, srow, grow, made, sem = refs[4:]
    for i in range(2):
        srow[i * 2 : i * 2 + 2] = specs[i][...].astype(F32)
        grow[i * 2 : i * 2 + 2] = grads[i][...].astype(F32)

    mask = mode_mask()
    low = lax.broadcasted_iota(jnp.int32, (32, 128), 1) < 64
    blank = jnp.zeros((64, 128), F32)

    def tall(ref, q, s, k, h):
        row = ref[s, q, k : k + 1, h * 256 : h * 256 + 256]
        return jnp.where(mask, jnp.broadcast_to(row, (8, 256)), 0.0)

    def copy_out(q):
        return pltpu.make_async_copy(made.at[q], out.at[q], sem.at[q])

    def step(q, carry):
        for h in range(2):
            sides = [
                jnp.concatenate(
                    [tall(grow, q, s, p * 16 + kx, h) for kx in range(MX) for s in range(4)], axis=0
                ).astype(BF)
                for p in range(2)
            ]
            pair = dot(jnp.concatenate(sides, axis=1), fold[...])
            for group in range(4):
                left = [
                    tall(srow, q, s, p * 16 + group * 4 + j, h)
                    for j in range(4)
                    for p in range(2)
                    for s in range(4)
                ]
                left = jnp.concatenate(left, axis=0).astype(BF)
                blocks = []
                for j in range(4):
                    at = (group * 4 + j) * 32
                    here = pair[at : at + 32]
                    there = jnp.concatenate([here[:, 64:], here[:, :64]], axis=1)
                    if j % 2 == 0:
                        one, two = jnp.where(low, here, 0.0), jnp.where(low, there, 0.0)
                    else:
                        one, two = jnp.where(low, 0.0, there), jnp.where(low, 0.0, here)
                    piece = jnp.concatenate([one, two], axis=0)
                    blocks.append(jnp.concatenate([piece, blank] if j < 2 else [blank, piece], axis=1))
                right = jnp.concatenate(blocks, axis=0).astype(BF)
                grad = lax.dot_general(
                    left, right, (((0,), (0,)), ((), ())), preferred_element_type=F32
                )
                for j in range(4):
                    at = group * 2048 + (j * 2 + h) * 256
                    made[q, at : at + 256, :] = grad[:, j * 64 : j * 64 + 64]
        copy_out(q).start()
        return carry

    lax.fori_loop(0, NQ, step, 0)
    for q in range(NQ):
        copy_out(q).wait()


def weight_gradient(specs, grads, t):
    return pl.pallas_call(
        weight_body,
        in_specs=[VM] * 5,
        out_specs=HBM,
        out_shape=jax.ShapeDtypeStruct((NQ, 8192, 64), F32),
        scratch_shapes=[pltpu.VMEM((4, NQ, 32, 512), F32), pltpu.VMEM((4, NQ, 32, 512), F32)]
        + [pltpu.VMEM((NQ, 8192, 64), F32), pltpu.SemaphoreType.DMA((NQ,))],
        name="weight_gradient",
        compiler_params=pltpu.CompilerParams(vmem_limit_bytes=52 << 20),
    )(*specs, *grads, t["fold"])


def exchange(values):
    return lax.all_to_all(values, "slab", split_axis=0, concat_axis=0, tiled=True)


def everyone(values):
    far = lax.ppermute(values, "dp", [(i, i ^ 2) for i in range(4)])
    both = jnp.stack([values, far])
    near = lax.ppermute(both, "dp", [(i, i ^ 1) for i in range(4)])
    return both, near


def per_device(field, cotangent, spectral_weight, point_weight, bias_term):
    t = tables()
    rows = field.reshape(4096, ZT)
    weights = spectral_weight.reshape(NQ, 8192, 64)
    sent = exchange(analyse(rows, t))
    lin = linear(rows, point_weight, bias_term, False)
    sent, lin = lax.optimization_barrier((sent, lin))
    back, spec = mix_forward(sent, weights, t)
    got = exchange(back)
    specs = everyone(spec)
    got, specs = lax.optimization_barrier((got, specs))
    act, grad_pre, out = activate(got, lin, cotangent.reshape(4096, ZT), t)
    sent = exchange(out)
    lin = linear(grad_pre, point_weight, None, True)
    sent, lin = lax.optimization_barrier((sent, lin))
    back, grad_spec = mix_backward(sent, weights, t)
    got = exchange(back)
    grads = everyone(grad_spec)
    weight_grad = weight_gradient(specs, grads, t).reshape(NQ, MX, MY, C, 2 * C)
    got, weight_grad = lax.optimization_barrier((got, weight_grad))
    total = finish(got, lin, t)
    shape = (1, 2, C, Y, ZT)
    return act.reshape(shape), total.reshape(shape), weight_grad


def solution(mesh):
    placed = (
        P("dp", "slab", None, None, None),
        P("dp", "slab", None, None, None),
        P("slab", None, None, None, None),
        P(),
        P(),
    )
    return jax.shard_map(
        per_device,
        mesh=mesh,
        in_specs=placed,
        out_specs=(
            P("dp", "slab", None, None, None),
            P("dp", "slab", None, None, None),
            P("slab", None, None, None, None),
        ),
        check_vma=False,
    )
```

```python
import math
from functools import partial

import jax
import jax.numpy as jnp
import numpy as np
from jax import lax
from jax.experimental import pallas as pl
from jax.experimental.pallas import tpu as pltpu
from jax.sharding import PartitionSpec as P


X = 64
Y = 64
Z = 32
T_SIZE = 16
ZT = Z * T_SIZE
C = 32
MX = 16
MY = 16
MZ = 12
MT = 8
NQ = 3
ND = 32
SCALE = 1.0 / (X * Y * Z * T_SIZE)
BF = jnp.bfloat16
F32 = jnp.float32


def signed(modes):
    i = np.arange(modes)
    return np.where(i < modes // 2, i, i - modes)


def inner_np():
    q = np.arange(MZ * MT)
    place = np.arange(ZT)
    kz = (signed(MZ)[q // MT] % Z)[:, None]
    kt = (q % MT)[:, None]
    counts = kz * (place // T_SIZE)[None] % Z * T_SIZE + kt * (place % T_SIZE)[None] % T_SIZE * Z
    angle = 2.0 * math.pi / ZT * (counts % ZT)
    return np.stack([np.cos(angle), -np.sin(angle)]).astype(np.float32)


def complex_np(modes, length):
    k = (signed(modes) % length)[:, None]
    angle = 2.0 * math.pi / length * (k * np.arange(length)[None] % length)
    c, s = np.cos(angle), np.sin(angle)
    return np.stack([np.stack([c, s], 1), np.stack([-s, c], 1)]).astype(np.float32)


def tables():
    inner = inner_np()
    mid = complex_np(MY, Y)
    out = complex_np(MX, X)
    depth = np.zeros((2, 128, ZT), np.float32)
    depth[:, :96] = inner.reshape(2, ND, NQ, ZT).transpose(0, 2, 1, 3).reshape(2, 96, ZT)
    depth = depth.reshape(256, ZT)
    middle = np.einsum("rkpy,cd->pcyrkd", mid, np.eye(8, dtype=np.float32)).reshape(1024, 256)
    eye4 = np.eye(4, dtype=np.float32)
    ana_out = np.einsum("rkpsi,gh->grkspih", out.reshape(2, MX, 2, ND, 2), eye4).reshape(128, 512)
    syn_out = out.reshape(2, MX, 2, ND, 2).transpose(2, 4, 3, 0, 1)
    fwd_out = np.repeat(syn_out.reshape(128, 32), 16, axis=1)
    bwd_out = np.repeat(syn_out.reshape(128, 32), 8, axis=1)
    spread = np.zeros((2, 2, 4, 8, 4, MY, 8), np.float32)
    for g in range(4):
        for c in range(8):
            spread[0, 0, g, c, g, :, c] = 1.0
            spread[1, 1, g, c, g, :, c] = 1.0
    spread = spread.reshape(2, 64, 512)
    fold = np.zeros((2, 8, C, 128), np.float32)
    for o in range(C):
        fold[0, :, o, o] = 1.0
        fold[0, :, o, 96 + o] = -1.0
        fold[1, :, o, 32 + o] = 1.0
        fold[1, :, o, 64 + o] = 1.0
    fold = fold.reshape(512, 128)
    t = dict(
        depth=depth, middle=middle, ana_out=ana_out, fwd_out=fwd_out * (SCALE / 2.0), bwd_out=bwd_out,
        spread=spread, fold=fold,
    )
    return {k: jnp.asarray(v, BF) for k, v in t.items()}


def dot(a, b):
    return lax.dot_general(a, b, (((1,), (0,)), ((), ())), preferred_element_type=F32)


def dot_t(a, b):
    return lax.dot_general(a, b, (((1,), (1,)), ((), ())), preferred_element_type=F32)


def owner_table(depth):
    return jnp.concatenate([depth[0:96, :], depth[128:224, :]], axis=0)


def analyse_rows(rows, slot, table, first):
    part = dot_t(table, rows).astype(BF)
    at = pl.ds(slot * 96, 96) if isinstance(slot, int) else pl.ds(pl.multiple_of(slot * 96, 32), 96)
    first[at, 0:512] = part[:96]
    first[at, 512:1024] = part[96:]


def by_owner(first, middle, out, work):
    second = dot(first[...], middle[...])
    for slot in range(8):
        for qi in range(NQ):
            for r in range(2):
                at = slot * 96 + qi * 32
                work[qi, pl.ds(r * 8 + slot, ND, stride=16), :] = second[
                    at : at + 32, r * 128 : r * 128 + 128
                ]
    for qi in range(NQ):
        out[:, qi * 16 : qi * 16 + 16, :] = work[qi].reshape(ND, 16, 128).astype(BF)


def chunk_copy(src, dst, sem, k):
    at = pl.ds(k * 512, 512)
    return pltpu.make_async_copy(src.at[at], dst.at[at], sem.at[k])


def analyse_body(v, depth_h, middle_h, out, have, first, work, depth, middle, sem, more):
    tables_in = [
        pltpu.make_async_copy(depth_h, depth, more.at[0]),
        pltpu.make_async_copy(middle_h, middle, more.at[1]),
    ]
    tables_in[0].start()
    for k in range(8):
        chunk_copy(v, have, sem, k).start()
    tables_in[1].start()
    tables_in[0].wait()
    table = owner_table(depth)
    for half in range(2):
        for k in range(half * 4, half * 4 + 4):
            chunk_copy(v, have, sem, k).wait()
        part = dot_t(table, have[half * 2048 : half * 2048 + 2048, :]).astype(BF)
        for k in range(4):
            at = half * 384 + k * 96
            first[at : at + 96, 0:512] = part[:96, k * 512 : k * 512 + 512]
            first[at : at + 96, 512:1024] = part[96:, k * 512 : k * 512 + 512]
    tables_in[1].wait()
    by_owner(first, middle, out, work)


HBM = pl.BlockSpec(memory_space=pltpu.HBM)
VM = pl.BlockSpec(memory_space=pltpu.VMEM)
GRID_ROWS = jax.ShapeDtypeStruct((4096, ZT), BF)
SENT = jax.ShapeDtypeStruct((ND, 48, 128), BF)


def analyse(values, t):
    return pl.pallas_call(
        analyse_body,
        in_specs=[HBM, HBM, HBM],
        out_specs=VM,
        out_shape=SENT,
        scratch_shapes=[
            pltpu.VMEM((4096, ZT), BF), pltpu.VMEM((768, 1024), BF),
            pltpu.VMEM((NQ, 512, 128), F32), pltpu.VMEM((256, ZT), BF), pltpu.VMEM((1024, 256), BF),
            pltpu.SemaphoreType.DMA((8,)), pltpu.SemaphoreType.DMA((2,)),
        ],
        name="analyse",
        compiler_params=pltpu.CompilerParams(vmem_limit_bytes=60 << 20),
    )(values, t["depth"], t["middle"])


def channel_order(perm):
    row = lax.broadcasted_iota(jnp.int32, (512, 512), 0)
    col = lax.broadcasted_iota(jnp.int32, (512, 512), 1)
    place = row // 8 % 16 * 32 + row // 128 * 8 + row % 8
    perm[...] = jnp.where(place == col, 1.0, 0.0).astype(BF)


def spectrum_rows(got, ana_out, perm, scale):
    tall = [got[:, q * 16 : q * 16 + 16, :].reshape(512, 128) for q in range(NQ)]
    parts = dot(ana_out[...], jnp.concatenate(tall, axis=1))
    if scale is not None:
        parts = parts * scale
    parts = parts.astype(BF)
    rows = [
        jnp.concatenate([parts[g * 32 : g * 32 + 32, q * 128 : q * 128 + 128] for g in range(4)], axis=1)
        for q in range(NQ)
    ]
    return dot(jnp.concatenate(rows, axis=0), perm[...])


def mode_mask():
    lane = lax.broadcasted_iota(jnp.int32, (8, 256), 1) // 32
    return lane == lax.broadcasted_iota(jnp.int32, (8, 256), 0)


def scatter_owner(synth, q, work, out):
    for r in range(2):
        for xi in range(2):
            for g in range(4):
                at = (r * 2 + xi) * 32
                work[q, pl.ds(r * 8 + xi * 4 + g, ND, stride=16), :] = synth[
                    at : at + 32, g * 128 : g * 128 + 128
                ]
    out[:, q * 16 : q * 16 + 16, :] = work[q].reshape(ND, 16, 128).astype(BF)


def weight_copy(w, have, sem, q):
    return pltpu.make_async_copy(w.at[q], have.at[q], sem.at[q])


def mix_forward_body(
    got, w, ana_out, spread, fwd_out, out, spec, have, srow, mixed, work, perm, sem
):
    for q in range(NQ):
        weight_copy(w, have, sem, q).start()
    channel_order(perm)
    rows = spectrum_rows(got, ana_out, perm, None)
    srow[...] = rows
    for q in range(NQ):
        spec[q] = rows[q * 32 : q * 32 + 32].astype(BF)
    mask = mode_mask()
    row_ky = lax.broadcasted_iota(jnp.int32, (256, 512), 0) % 16
    lane_ky = lax.broadcasted_iota(jnp.int32, (256, 512), 1) // 8 % 16
    same = row_ky == lane_ky
    for q in range(NQ):
        weight_copy(w, have, sem, q).wait()
        for kx in range(MX):
            for h in range(2):
                lanes = slice(h * 256, h * 256 + 256)
                at = q * 32 + kx
                real = jnp.where(mask, jnp.broadcast_to(srow[at : at + 1, lanes], (8, 256)), 0.0)
                at = at + 16
                imag = jnp.where(mask, jnp.broadcast_to(srow[at : at + 1, lanes], (8, 256)), 0.0)
                left = jnp.concatenate([real, imag], axis=0).astype(BF)
                at = (kx * 2 + h) * 256
                both = dot(left, have[q, at : at + 256, :])
                low = both[8:16]
                turned = jnp.concatenate([-low[:, 32:], low[:, :32]], axis=1)
                at = kx * 16 + h * 8
                mixed[q, at : at + 8, :] = both[:8] + turned
        values = mixed[q].astype(BF)
        wide = [jnp.where(same, dot(values, spread[p]), 0.0).astype(BF) for p in range(2)]
        synth = dot(fwd_out[...], jnp.concatenate(wide, axis=0))
        scatter_owner(synth, q, work, out)


SPECTRUM = jax.ShapeDtypeStruct((NQ, 32, 512), BF)


def mix_forward(got, weights, t):
    return pl.pallas_call(
        mix_forward_body,
        in_specs=[VM, HBM, VM, VM, VM],
        out_specs=[VM, VM],
        out_shape=[SENT, SPECTRUM],
        scratch_shapes=[
            pltpu.VMEM((NQ, 8192, 64), BF), pltpu.VMEM((96, 512), F32), pltpu.VMEM((NQ, 256, 64), F32),
            pltpu.VMEM((NQ, 512, 128), F32), pltpu.VMEM((512, 512), BF),
            pltpu.SemaphoreType.DMA((NQ,)),
        ],
        name="mix_forward",
        compiler_params=pltpu.CompilerParams(vmem_limit_bytes=52 << 20),
    )(got, weights, t["ana_out"], t["spread"], t["fwd_out"])


def mix_backward_body(
    got, w, ana_out, fold, bwd_out, out, spec, have, srow, pair, masked, work, perm, sem
):
    for q in range(NQ):
        weight_copy(w, have, sem, q).start()
    channel_order(perm)
    rows = spectrum_rows(got, ana_out, perm, SCALE / 2.0)
    srow[...] = rows
    for q in range(NQ):
        spec[q] = rows[q * 32 : q * 32 + 32].astype(BF)
    mask = mode_mask()
    for h in range(2):
        lanes = slice(h * 256, h * 256 + 256)
        sides = []
        for part in range(2):
            tall = [
                jnp.where(mask, jnp.broadcast_to(srow[k : k + 1, lanes], (8, 256)), 0.0)
                for q in range(NQ)
                for k in range(q * 32 + part * 16, q * 32 + part * 16 + 16)
            ]
            sides.append(jnp.concatenate(tall, axis=0).astype(BF))
        pair[h] = dot(jnp.concatenate(sides, axis=1), fold[...])
    for q in range(NQ):
        weight_copy(w, have, sem, q).wait()
        for kx in range(MX):
            for h in range(2):
                at = q * 128 + kx * 8
                both = pair[h, at : at + 8, :]
                left = jnp.concatenate([both[:, :64], both[:, 64:]], axis=0).astype(BF)
                at = (kx * 2 + h) * 256
                full = dot_t(left, have[q, at : at + 256, :])
                masked[q, h, kx * 8 : kx * 8 + 8, :] = jnp.where(mask, full[:8], 0.0)
                masked[q, h, 128 + kx * 8 : 136 + kx * 8, :] = jnp.where(mask, full[8:], 0.0)
        synth = [dot(bwd_out[...], masked[q, h].astype(BF)).astype(BF) for h in range(2)]
        turned = dot_t(jnp.concatenate(synth, axis=1), perm[...])
        scatter_owner(turned, q, work, out)


def mix_backward(got, weights, t):
    return pl.pallas_call(
        mix_backward_body,
        in_specs=[VM, HBM, VM, VM, VM],
        out_specs=[VM, VM],
        out_shape=[SENT, SPECTRUM],
        scratch_shapes=[
            pltpu.VMEM((NQ, 8192, 64), BF), pltpu.VMEM((96, 512), F32), pltpu.VMEM((2, 384, 128), F32),
            pltpu.VMEM((NQ, 2, 256, 256), F32), pltpu.VMEM((NQ, 512, 128), F32),
            pltpu.VMEM((512, 512), BF), pltpu.SemaphoreType.DMA((NQ,)),
        ],
        name="mix_backward",
        compiler_params=pltpu.CompilerParams(vmem_limit_bytes=52 << 20),
    )(got, weights, t["ana_out"], t["fold"], t["bwd_out"])


def unpack(got, have, turned, middle, tall):
    for qi in range(NQ):
        have[qi] = got[:, qi * 16 : qi * 16 + 16, :].reshape(512, 128).astype(F32)
    for slot in range(8):
        for p in range(2):
            pieces = [have[qi, pl.ds(p * 8 + slot, ND, stride=16), :] for qi in range(NQ)]
            pieces.append(jnp.zeros((ND, 128), F32))
            turned[slot * 128 : slot * 128 + 128, p * 128 : p * 128 + 128] = jnp.concatenate(
                pieces, axis=0
            ).astype(BF)
    for r in range(2):
        block = dot_t(middle[r * 512 : r * 512 + 512, :], turned[...]).astype(BF)
        for slot in range(8):
            tall[slot * 512 : slot * 512 + 512, r * 128 : r * 128 + 128] = block[
                :, slot * 128 : slot * 128 + 128
            ]


ROOT = math.sqrt(2.0 / math.pi)


def activate_body(
    got, lin, cot, depth, middle, act, grad, out, lin_v, cot_v, act_v, grad_v, have, turned, tall,
    first, work, sems,
):
    for k in range(8):
        chunk_copy(lin, lin_v, sems.at[0], k).start()
        chunk_copy(cot, cot_v, sems.at[1], k).start()
    grad_v[0:512, :] = jnp.zeros((512, ZT), BF)
    unpack(got, have, turned, middle, tall)
    table = owner_table(depth)

    def grad_copy(k):
        at = pl.ds(k * 512, 512)
        return pltpu.make_async_copy(grad_v.at[pl.ds(k * 512 + 512, 512)], grad.at[at], sems.at[3, k])

    def step(i, carry):
        base = pl.multiple_of(i * 1024, 1024)
        for u in range(2):
            chunk_copy(lin, lin_v, sems.at[0], i * 2 + u).wait()
            chunk_copy(cot, cot_v, sems.at[1], i * 2 + u).wait()
        for u in range(2):
            rows = grad_v[pl.ds(base + u * 512, 512), :]
            slot = jnp.maximum(i * 2 + u - 1, 0)
            analyse_rows(rows, slot, table, first)
            at = pl.ds(base + u * 512, 512)
            w = dot(tall[at, :], depth[...]) + lin_v[at, :].astype(F32)
            square = w * w
            t = jnp.tanh(w * (2.0 * ROOT + (8.0 * ROOT * 0.044715) * square))
            one = 1.0 + t
            value = w * one
            slope = one + value * (1.0 - t) * (2.0 * ROOT + (24.0 * ROOT * 0.044715) * square)
            act_v[at, :] = value.astype(BF)
            grad_v[pl.ds(base + u * 512 + 512, 512), :] = cot_v[at, :] * slope.astype(BF)
            chunk_copy(act_v, act, sems.at[2], i * 2 + u).start()
            grad_copy(i * 2 + u).start()
        return carry

    lax.fori_loop(0, 4, step, 0)
    analyse_rows(grad_v[4096:4608, :], 7, table, first)
    by_owner(first, middle, out, work)
    for k in range(8):
        chunk_copy(act_v, act, sems.at[2], k).wait()
        grad_copy(k).wait()


SYNTH_SCRATCH = [
    pltpu.VMEM((NQ, 512, 128), F32), pltpu.VMEM((1024, 256), BF), pltpu.VMEM((4096, 256), BF),
]


def activate(got, lin, cot, t):
    return pl.pallas_call(
        activate_body,
        in_specs=[VM, HBM, HBM, VM, VM],
        out_specs=[HBM, HBM, VM],
        out_shape=[GRID_ROWS, GRID_ROWS, SENT],
        scratch_shapes=[pltpu.VMEM((4096, ZT), BF)] * 3
        + [pltpu.VMEM((4608, ZT), BF)]
        + SYNTH_SCRATCH
        + [
            pltpu.VMEM((768, 1024), BF), pltpu.VMEM((NQ, 512, 128), F32),
            pltpu.SemaphoreType.DMA((4, 8)),
        ],
        name="activate",
        compiler_params=pltpu.CompilerParams(vmem_limit_bytes=52 << 20),
    )(got, lin, cot, t["depth"], t["middle"])


def finish_body(got, lin, depth, middle, out, lin_v, out_v, have, turned, tall, sems):
    for k in range(8):
        chunk_copy(lin, lin_v, sems.at[0], k).start()
    unpack(got, have, turned, middle, tall)

    def step(k, carry):
        chunk_copy(lin, lin_v, sems.at[0], k).wait()
        at = pl.ds(pl.multiple_of(k * 512, 512), 512)
        out_v[at, :] = (dot(tall[at, :], depth[...]) + lin_v[at, :].astype(F32)).astype(BF)
        chunk_copy(out_v, out, sems.at[1], k).start()
        return carry

    lax.fori_loop(0, 8, step, 0)
    for k in range(8):
        chunk_copy(out_v, out, sems.at[1], k).wait()


def finish(got, lin, t):
    return pl.pallas_call(
        finish_body,
        in_specs=[VM, HBM, VM, VM],
        out_specs=HBM,
        out_shape=GRID_ROWS,
        scratch_shapes=[pltpu.VMEM((4096, ZT), BF)] * 2
        + SYNTH_SCRATCH
        + [pltpu.SemaphoreType.DMA((2, 8))],
        name="finish",
        compiler_params=pltpu.CompilerParams(vmem_limit_bytes=52 << 20),
    )(got, lin, t["depth"], t["middle"])


def linear_body(turn, v, matrix, bias, out, have, made, kron, sems):
    for k in range(8):
        chunk_copy(v, have, sems.at[0], k).start()
    rows = lax.broadcasted_iota(jnp.int32, (512, C), 0) // 16
    pick = jnp.where(rows == lax.broadcasted_iota(jnp.int32, (512, C), 1), 1.0, 0.0).astype(BF)
    if turn:
        wide = lax.dot_general(matrix[...], pick, (((0,), (1,)), ((), ())), preferred_element_type=F32)
    else:
        wide = dot_t(matrix[...], pick)
    tall = dot(pick, wide.astype(BF))
    row = lax.broadcasted_iota(jnp.int32, (512, 512), 0) % 16
    col = lax.broadcasted_iota(jnp.int32, (512, 512), 1) % 16
    kron[...] = jnp.where(row == col, tall * 0.5, 0.0).astype(BF)
    for x in range(2):
        for k in range(4):
            chunk_copy(v, have, sems.at[0], x * 4 + k).wait()
        grid = have.at[pl.ds(x * 2048, 2048)].reshape(C, Y, ZT)
        done = made.at[pl.ds(x * 2048, 2048)].reshape(C, Y, ZT)
        for g in range(4):
            cells = grid[:, g * 16 : g * 16 + 16, :].reshape(512, ZT)
            result = dot(kron[...], cells)
            for c in range(C):
                one = result[c * 16 : c * 16 + 16]
                if bias is not None:
                    one = one + 0.5 * bias[c]
                done[c, g * 16 : g * 16 + 16, :] = one.astype(BF)
        for k in range(4):
            chunk_copy(made, out, sems.at[1], x * 4 + k).start()
    for k in range(8):
        chunk_copy(made, out, sems.at[1], k).wait()


def linear(values, matrix, bias, turn):
    if bias is None:
        body = lambda v, m, *rest: linear_body(turn, v, m, None, *rest)
        more = []
    else:
        body = partial(linear_body, turn)
        more = [bias]
    return pl.pallas_call(
        body,
        in_specs=[HBM, VM] + [pl.BlockSpec(memory_space=pltpu.SMEM)] * len(more),
        out_specs=HBM,
        out_shape=GRID_ROWS,
        scratch_shapes=[
            pltpu.VMEM((4096, ZT), BF), pltpu.VMEM((4096, ZT), BF), pltpu.VMEM((512, 512), BF),
            pltpu.SemaphoreType.DMA((2, 8)),
        ],
        name="linear",
        compiler_params=pltpu.CompilerParams(vmem_limit_bytes=52 << 20),
    )(values, matrix, *more)


def weight_body(*refs):
    specs, grads = refs[:2], refs[2:4]
    fold, out, srow, grow, made, sem = refs[4:]
    for i in range(2):
        srow[i * 2 : i * 2 + 2] = specs[i][...].astype(F32)
        grow[i * 2 : i * 2 + 2] = grads[i][...].astype(F32)

    mask = mode_mask()
    low = lax.broadcasted_iota(jnp.int32, (32, 128), 1) < 64
    blank = jnp.zeros((64, 128), F32)

    def tall(ref, q, s, k, h):
        row = ref[s, q, k : k + 1, h * 256 : h * 256 + 256]
        return jnp.where(mask, jnp.broadcast_to(row, (8, 256)), 0.0)

    def copy_out(q):
        return pltpu.make_async_copy(made.at[q], out.at[q], sem.at[q])

    def step(q, carry):
        for h in range(2):
            sides = [
                jnp.concatenate(
                    [tall(grow, q, s, p * 16 + kx, h) for kx in range(MX) for s in range(4)], axis=0
                ).astype(BF)
                for p in range(2)
            ]
            pair = dot(jnp.concatenate(sides, axis=1), fold[...])
            for group in range(4):
                left = [
                    tall(srow, q, s, p * 16 + group * 4 + j, h)
                    for j in range(4)
                    for p in range(2)
                    for s in range(4)
                ]
                left = jnp.concatenate(left, axis=0).astype(BF)
                blocks = []
                for j in range(4):
                    at = (group * 4 + j) * 32
                    here = pair[at : at + 32]
                    there = jnp.concatenate([here[:, 64:], here[:, :64]], axis=1)
                    if j % 2 == 0:
                        one, two = jnp.where(low, here, 0.0), jnp.where(low, there, 0.0)
                    else:
                        one, two = jnp.where(low, 0.0, there), jnp.where(low, 0.0, here)
                    piece = jnp.concatenate([one, two], axis=0)
                    blocks.append(jnp.concatenate([piece, blank] if j < 2 else [blank, piece], axis=1))
                right = jnp.concatenate(blocks, axis=0).astype(BF)
                grad = lax.dot_general(
                    left, right, (((0,), (0,)), ((), ())), preferred_element_type=F32
                )
                for j in range(4):
                    at = group * 2048 + (j * 2 + h) * 256
                    made[q, at : at + 256, :] = grad[:, j * 64 : j * 64 + 64]
        copy_out(q).start()
        return carry

    lax.fori_loop(0, NQ, step, 0)
    for q in range(NQ):
        copy_out(q).wait()


def weight_gradient(specs, grads, t):
    return pl.pallas_call(
        weight_body,
        in_specs=[VM] * 5,
        out_specs=HBM,
        out_shape=jax.ShapeDtypeStruct((NQ, 8192, 64), F32),
        scratch_shapes=[pltpu.VMEM((4, NQ, 32, 512), F32), pltpu.VMEM((4, NQ, 32, 512), F32)]
        + [pltpu.VMEM((NQ, 8192, 64), F32), pltpu.SemaphoreType.DMA((NQ,))],
        name="weight_gradient",
        compiler_params=pltpu.CompilerParams(vmem_limit_bytes=52 << 20),
    )(*specs, *grads, t["fold"])


def exchange(values):
    return lax.all_to_all(values, "slab", split_axis=0, concat_axis=0, tiled=True)


def everyone(values):
    far = lax.ppermute(values, "dp", [(i, i ^ 2) for i in range(4)])
    both = jnp.stack([values, far])
    near = lax.ppermute(both, "dp", [(i, i ^ 1) for i in range(4)])
    return both, near


def layer(field, cotangent, spectral_weight, point_weight, bias_term):
    t = tables()
    rows = field.reshape(4096, ZT)
    weights = spectral_weight.reshape(NQ, 8192, 64)
    sent = exchange(analyse(rows, t))
    lin = linear(rows, point_weight, bias_term, False)
    sent, lin = lax.optimization_barrier((sent, lin))
    back, spec = mix_forward(sent, weights, t)
    got = exchange(back)
    specs = everyone(spec)
    got, specs = lax.optimization_barrier((got, specs))
    act, grad_pre, out = activate(got, lin, cotangent.reshape(4096, ZT), t)
    sent = exchange(out)
    lin = linear(grad_pre, point_weight, None, True)
    sent, lin = lax.optimization_barrier((sent, lin))
    back, grad_spec = mix_backward(sent, weights, t)
    got = exchange(back)
    grads = everyone(grad_spec)
    weight_grad = weight_gradient(specs, grads, t).reshape(NQ, MX, MY, C, 2 * C)
    got, weight_grad = lax.optimization_barrier((got, weight_grad))
    total = finish(got, lin, t)
    shape = (1, 2, C, Y, ZT)
    return act.reshape(shape), total.reshape(shape), weight_grad


def solution(mesh):
    placed = (
        P("dp", "slab", None, None, None),
        P("dp", "slab", None, None, None),
        P("slab", None, None, None, None),
        P(),
        P(),
    )
    return jax.shard_map(
        layer,
        mesh=mesh,
        in_specs=placed,
        out_specs=(
            P("dp", "slab", None, None, None),
            P("dp", "slab", None, None, None),
            P("slab", None, None, None, None),
        ),
        check_vma=False,
    )
```

```python
import math
from functools import partial

import jax
import jax.numpy as jnp
import numpy as np
from jax import lax
from jax.experimental import pallas as pl
from jax.experimental.pallas import tpu as pltpu
from jax.sharding import PartitionSpec as P


X = 64
Y = 64
Z = 32
T_SIZE = 16
ZT = Z * T_SIZE
C = 32
MX = 16
MY = 16
MZ = 12
MT = 8
NQ = 3
ND = 32
SCALE = 1.0 / (X * Y * Z * T_SIZE)
BF = jnp.bfloat16
F32 = jnp.float32


def signed(modes):
    i = np.arange(modes)
    return np.where(i < modes // 2, i, i - modes)


def inner_np():
    q = np.arange(MZ * MT)
    place = np.arange(ZT)
    kz = (signed(MZ)[q // MT] % Z)[:, None]
    kt = (q % MT)[:, None]
    counts = kz * (place // T_SIZE)[None] % Z * T_SIZE + kt * (place % T_SIZE)[None] % T_SIZE * Z
    angle = 2.0 * math.pi / ZT * (counts % ZT)
    return np.stack([np.cos(angle), -np.sin(angle)]).astype(np.float32)


def complex_np(modes, length):
    k = (signed(modes) % length)[:, None]
    angle = 2.0 * math.pi / length * (k * np.arange(length)[None] % length)
    c, s = np.cos(angle), np.sin(angle)
    return np.stack([np.stack([c, s], 1), np.stack([-s, c], 1)]).astype(np.float32)


def tables():
    inner = inner_np()
    mid = complex_np(MY, Y)
    out = complex_np(MX, X)
    depth = np.zeros((2, 128, ZT), np.float32)
    depth[:, :96] = inner.reshape(2, ND, NQ, ZT).transpose(0, 2, 1, 3).reshape(2, 96, ZT)
    depth = depth.reshape(256, ZT)
    middle = np.einsum("rkpy,cd->pcyrkd", mid, np.eye(8, dtype=np.float32)).reshape(1024, 256)
    eye4 = np.eye(4, dtype=np.float32)
    ana_out = np.einsum("rkpsi,gh->grkspih", out.reshape(2, MX, 2, ND, 2), eye4).reshape(128, 512)
    syn_out = out.reshape(2, MX, 2, ND, 2).transpose(2, 4, 3, 0, 1)
    fwd_out = np.repeat(syn_out.reshape(128, 32), 16, axis=1)
    bwd_out = np.repeat(syn_out.reshape(128, 32), 8, axis=1)
    spread = np.zeros((2, 2, 4, 8, 4, MY, 8), np.float32)
    for g in range(4):
        for c in range(8):
            spread[0, 0, g, c, g, :, c] = 1.0
            spread[1, 1, g, c, g, :, c] = 1.0
    spread = spread.reshape(2, 64, 512)
    fold = np.zeros((2, 8, C, 128), np.float32)
    for o in range(C):
        fold[0, :, o, o] = 1.0
        fold[0, :, o, 96 + o] = -1.0
        fold[1, :, o, 32 + o] = 1.0
        fold[1, :, o, 64 + o] = 1.0
    fold = fold.reshape(512, 128)
    t = dict(
        depth=depth, middle=middle, ana_out=ana_out, fwd_out=fwd_out * (SCALE / 2.0), bwd_out=bwd_out,
        spread=spread, fold=fold,
    )
    return {k: jnp.asarray(v, BF) for k, v in t.items()}


def dot(a, b):
    return lax.dot_general(a, b, (((1,), (0,)), ((), ())), preferred_element_type=F32)


def dot_t(a, b):
    return lax.dot_general(a, b, (((1,), (1,)), ((), ())), preferred_element_type=F32)


def owner_table(depth):
    return jnp.concatenate([depth[0:96, :], depth[128:224, :]], axis=0)


def analyse_rows(rows, slot, table, first):
    part = dot_t(table, rows).astype(BF)
    at = pl.ds(slot * 96, 96) if isinstance(slot, int) else pl.ds(pl.multiple_of(slot * 96, 32), 96)
    first[at, 0:512] = part[:96]
    first[at, 512:1024] = part[96:]


def by_owner(first, middle, out, work):
    second = dot(first[...], middle[...])
    for slot in range(8):
        for qi in range(NQ):
            for r in range(2):
                at = slot * 96 + qi * 32
                work[qi, pl.ds(r * 8 + slot, ND, stride=16), :] = second[
                    at : at + 32, r * 128 : r * 128 + 128
                ]
    for qi in range(NQ):
        out[:, qi * 16 : qi * 16 + 16, :] = work[qi].reshape(ND, 16, 128).astype(BF)


def chunk_copy(src, dst, sem, k):
    at = pl.ds(k * 512, 512)
    return pltpu.make_async_copy(src.at[at], dst.at[at], sem.at[k])


def analyse_body(v, depth_h, middle_h, out, have, first, work, depth, middle, sem, more):
    tables_in = [
        pltpu.make_async_copy(depth_h, depth, more.at[0]),
        pltpu.make_async_copy(middle_h, middle, more.at[1]),
    ]
    tables_in[0].start()
    for k in range(8):
        chunk_copy(v, have, sem, k).start()
    tables_in[1].start()
    tables_in[0].wait()
    table = owner_table(depth)
    for half in range(2):
        for k in range(half * 4, half * 4 + 4):
            chunk_copy(v, have, sem, k).wait()
        part = dot_t(table, have[half * 2048 : half * 2048 + 2048, :]).astype(BF)
        for k in range(4):
            at = half * 384 + k * 96
            first[at : at + 96, 0:512] = part[:96, k * 512 : k * 512 + 512]
            first[at : at + 96, 512:1024] = part[96:, k * 512 : k * 512 + 512]
    tables_in[1].wait()
    by_owner(first, middle, out, work)


HBM = pl.BlockSpec(memory_space=pltpu.HBM)
VM = pl.BlockSpec(memory_space=pltpu.VMEM)
GRID_ROWS = jax.ShapeDtypeStruct((4096, ZT), BF)
SENT = jax.ShapeDtypeStruct((ND, 48, 128), BF)


def analyse(values, t):
    return pl.pallas_call(
        analyse_body,
        in_specs=[HBM, HBM, HBM],
        out_specs=VM,
        out_shape=SENT,
        scratch_shapes=[
            pltpu.VMEM((4096, ZT), BF), pltpu.VMEM((768, 1024), BF),
            pltpu.VMEM((NQ, 512, 128), F32), pltpu.VMEM((256, ZT), BF), pltpu.VMEM((1024, 256), BF),
            pltpu.SemaphoreType.DMA((8,)), pltpu.SemaphoreType.DMA((2,)),
        ],
        name="analyse",
        compiler_params=pltpu.CompilerParams(vmem_limit_bytes=60 << 20),
    )(values, t["depth"], t["middle"])


def channel_order(perm):
    row = lax.broadcasted_iota(jnp.int32, (512, 512), 0)
    col = lax.broadcasted_iota(jnp.int32, (512, 512), 1)
    place = row // 8 % 16 * 32 + row // 128 * 8 + row % 8
    perm[...] = jnp.where(place == col, 1.0, 0.0).astype(BF)


def spectrum_rows(got, ana_out, perm, scale):
    tall = [got[:, q * 16 : q * 16 + 16, :].reshape(512, 128) for q in range(NQ)]
    parts = dot(ana_out[...], jnp.concatenate(tall, axis=1))
    if scale is not None:
        parts = parts * scale
    parts = parts.astype(BF)
    rows = [
        jnp.concatenate([parts[g * 32 : g * 32 + 32, q * 128 : q * 128 + 128] for g in range(4)], axis=1)
        for q in range(NQ)
    ]
    return dot(jnp.concatenate(rows, axis=0), perm[...])


def mode_mask():
    lane = lax.broadcasted_iota(jnp.int32, (8, 256), 1) // 32
    return lane == lax.broadcasted_iota(jnp.int32, (8, 256), 0)


def scatter_owner(synth, q, work, out):
    for r in range(2):
        for xi in range(2):
            for g in range(4):
                at = (r * 2 + xi) * 32
                work[q, pl.ds(r * 8 + xi * 4 + g, ND, stride=16), :] = synth[
                    at : at + 32, g * 128 : g * 128 + 128
                ]
    out[:, q * 16 : q * 16 + 16, :] = work[q].reshape(ND, 16, 128).astype(BF)


def weight_copy(w, have, sem, q):
    return pltpu.make_async_copy(w.at[q], have.at[q], sem.at[q])


def mix_forward_body(
    got, w, ana_out, spread, fwd_out, out, spec, have, srow, mixed, work, perm, sem
):
    for q in range(NQ):
        weight_copy(w, have, sem, q).start()
    channel_order(perm)
    rows = spectrum_rows(got, ana_out, perm, None)
    srow[...] = rows
    for q in range(NQ):
        spec[q] = rows[q * 32 : q * 32 + 32].astype(BF)
    mask = mode_mask()
    row_ky = lax.broadcasted_iota(jnp.int32, (256, 512), 0) % 16
    lane_ky = lax.broadcasted_iota(jnp.int32, (256, 512), 1) // 8 % 16
    same = row_ky == lane_ky
    for q in range(NQ):
        weight_copy(w, have, sem, q).wait()
        for kx in range(MX):
            for h in range(2):
                lanes = slice(h * 256, h * 256 + 256)
                at = q * 32 + kx
                real = jnp.where(mask, jnp.broadcast_to(srow[at : at + 1, lanes], (8, 256)), 0.0)
                at = at + 16
                imag = jnp.where(mask, jnp.broadcast_to(srow[at : at + 1, lanes], (8, 256)), 0.0)
                left = jnp.concatenate([real, imag], axis=0).astype(BF)
                at = (kx * 2 + h) * 256
                both = dot(left, have[q, at : at + 256, :])
                low = both[8:16]
                turned = jnp.concatenate([-low[:, 32:], low[:, :32]], axis=1)
                at = kx * 16 + h * 8
                mixed[q, at : at + 8, :] = both[:8] + turned
        values = mixed[q].astype(BF)
        wide = [jnp.where(same, dot(values, spread[p]), 0.0).astype(BF) for p in range(2)]
        synth = dot(fwd_out[...], jnp.concatenate(wide, axis=0))
        scatter_owner(synth, q, work, out)


SPECTRUM = jax.ShapeDtypeStruct((NQ, 32, 512), BF)


def mix_forward(got, weights, t):
    return pl.pallas_call(
        mix_forward_body,
        in_specs=[VM, HBM, VM, VM, VM],
        out_specs=[VM, VM],
        out_shape=[SENT, SPECTRUM],
        scratch_shapes=[
            pltpu.VMEM((NQ, 8192, 64), BF), pltpu.VMEM((96, 512), F32), pltpu.VMEM((NQ, 256, 64), F32),
            pltpu.VMEM((NQ, 512, 128), F32), pltpu.VMEM((512, 512), BF),
            pltpu.SemaphoreType.DMA((NQ,)),
        ],
        name="mix_forward",
        compiler_params=pltpu.CompilerParams(vmem_limit_bytes=52 << 20),
    )(got, weights, t["ana_out"], t["spread"], t["fwd_out"])


def mix_backward_body(
    got, w, ana_out, fold, bwd_out, out, spec, have, srow, pair, masked, work, perm, sem
):
    for q in range(NQ):
        weight_copy(w, have, sem, q).start()
    channel_order(perm)
    rows = spectrum_rows(got, ana_out, perm, SCALE / 2.0)
    srow[...] = rows
    for q in range(NQ):
        spec[q] = rows[q * 32 : q * 32 + 32].astype(BF)
    mask = mode_mask()
    for h in range(2):
        lanes = slice(h * 256, h * 256 + 256)
        sides = []
        for part in range(2):
            tall = [
                jnp.where(mask, jnp.broadcast_to(srow[k : k + 1, lanes], (8, 256)), 0.0)
                for q in range(NQ)
                for k in range(q * 32 + part * 16, q * 32 + part * 16 + 16)
            ]
            sides.append(jnp.concatenate(tall, axis=0).astype(BF))
        pair[h] = dot(jnp.concatenate(sides, axis=1), fold[...])
    for q in range(NQ):
        weight_copy(w, have, sem, q).wait()
        for kx in range(MX):
            for h in range(2):
                at = q * 128 + kx * 8
                both = pair[h, at : at + 8, :]
                left = jnp.concatenate([both[:, :64], both[:, 64:]], axis=0).astype(BF)
                at = (kx * 2 + h) * 256
                full = dot_t(left, have[q, at : at + 256, :])
                masked[q, h, kx * 8 : kx * 8 + 8, :] = jnp.where(mask, full[:8], 0.0)
                masked[q, h, 128 + kx * 8 : 136 + kx * 8, :] = jnp.where(mask, full[8:], 0.0)
        synth = [dot(bwd_out[...], masked[q, h].astype(BF)).astype(BF) for h in range(2)]
        turned = dot_t(jnp.concatenate(synth, axis=1), perm[...])
        scatter_owner(turned, q, work, out)


def mix_backward(got, weights, t):
    return pl.pallas_call(
        mix_backward_body,
        in_specs=[VM, HBM, VM, VM, VM],
        out_specs=[VM, VM],
        out_shape=[SENT, SPECTRUM],
        scratch_shapes=[
            pltpu.VMEM((NQ, 8192, 64), BF), pltpu.VMEM((96, 512), F32), pltpu.VMEM((2, 384, 128), F32),
            pltpu.VMEM((NQ, 2, 256, 256), F32), pltpu.VMEM((NQ, 512, 128), F32),
            pltpu.VMEM((512, 512), BF), pltpu.SemaphoreType.DMA((NQ,)),
        ],
        name="mix_backward",
        compiler_params=pltpu.CompilerParams(vmem_limit_bytes=52 << 20),
    )(got, weights, t["ana_out"], t["fold"], t["bwd_out"])


def unpack(got, have, turned, middle, tall):
    for qi in range(NQ):
        have[qi] = got[:, qi * 16 : qi * 16 + 16, :].reshape(512, 128).astype(F32)
    for slot in range(8):
        for p in range(2):
            pieces = [have[qi, pl.ds(p * 8 + slot, ND, stride=16), :] for qi in range(NQ)]
            pieces.append(jnp.zeros((ND, 128), F32))
            turned[slot * 128 : slot * 128 + 128, p * 128 : p * 128 + 128] = jnp.concatenate(
                pieces, axis=0
            ).astype(BF)
    for r in range(2):
        block = dot_t(middle[r * 512 : r * 512 + 512, :], turned[...]).astype(BF)
        for slot in range(8):
            tall[slot * 512 : slot * 512 + 512, r * 128 : r * 128 + 128] = block[
                :, slot * 128 : slot * 128 + 128
            ]


ROOT = math.sqrt(2.0 / math.pi)


def activate_body(
    got, lin, cot, depth, middle, act, grad, out, lin_v, cot_v, act_v, grad_v, have, turned, tall,
    first, work, sems,
):
    for k in range(8):
        chunk_copy(lin, lin_v, sems.at[0], k).start()
        chunk_copy(cot, cot_v, sems.at[1], k).start()
    grad_v[0:512, :] = jnp.zeros((512, ZT), BF)
    unpack(got, have, turned, middle, tall)
    table = owner_table(depth)

    def grad_copy(k):
        at = pl.ds(k * 512, 512)
        return pltpu.make_async_copy(grad_v.at[pl.ds(k * 512 + 512, 512)], grad.at[at], sems.at[3, k])

    def step(i, carry):
        base = pl.multiple_of(i * 1024, 1024)
        for u in range(2):
            chunk_copy(lin, lin_v, sems.at[0], i * 2 + u).wait()
            chunk_copy(cot, cot_v, sems.at[1], i * 2 + u).wait()
        for u in range(2):
            rows = grad_v[pl.ds(base + u * 512, 512), :]
            slot = jnp.maximum(i * 2 + u - 1, 0)
            analyse_rows(rows, slot, table, first)
            at = pl.ds(base + u * 512, 512)
            w = dot(tall[at, :], depth[...]) + lin_v[at, :].astype(F32)
            square = w * w
            t = jnp.tanh(w * (2.0 * ROOT + (8.0 * ROOT * 0.044715) * square))
            one = 1.0 + t
            value = w * one
            slope = one + value * (1.0 - t) * (2.0 * ROOT + (24.0 * ROOT * 0.044715) * square)
            act_v[at, :] = value.astype(BF)
            grad_v[pl.ds(base + u * 512 + 512, 512), :] = cot_v[at, :] * slope.astype(BF)
            chunk_copy(act_v, act, sems.at[2], i * 2 + u).start()
            grad_copy(i * 2 + u).start()
        return carry

    lax.fori_loop(0, 4, step, 0)
    analyse_rows(grad_v[4096:4608, :], 7, table, first)
    by_owner(first, middle, out, work)
    for k in range(8):
        chunk_copy(act_v, act, sems.at[2], k).wait()
        grad_copy(k).wait()


SYNTH_SCRATCH = [
    pltpu.VMEM((NQ, 512, 128), F32), pltpu.VMEM((1024, 256), BF), pltpu.VMEM((4096, 256), BF),
]


def activate(got, lin, cot, t):
    return pl.pallas_call(
        activate_body,
        in_specs=[VM, HBM, HBM, VM, VM],
        out_specs=[HBM, HBM, VM],
        out_shape=[GRID_ROWS, GRID_ROWS, SENT],
        scratch_shapes=[pltpu.VMEM((4096, ZT), BF)] * 3
        + [pltpu.VMEM((4608, ZT), BF)]
        + SYNTH_SCRATCH
        + [
            pltpu.VMEM((768, 1024), BF), pltpu.VMEM((NQ, 512, 128), F32),
            pltpu.SemaphoreType.DMA((4, 8)),
        ],
        name="activate",
        compiler_params=pltpu.CompilerParams(vmem_limit_bytes=52 << 20),
    )(got, lin, cot, t["depth"], t["middle"])


def finish_body(got, lin, depth, middle, out, lin_v, out_v, have, turned, tall, sems):
    for k in range(8):
        chunk_copy(lin, lin_v, sems.at[0], k).start()
    unpack(got, have, turned, middle, tall)

    def step(k, carry):
        chunk_copy(lin, lin_v, sems.at[0], k).wait()
        at = pl.ds(pl.multiple_of(k * 512, 512), 512)
        out_v[at, :] = (dot(tall[at, :], depth[...]) + lin_v[at, :].astype(F32)).astype(BF)
        chunk_copy(out_v, out, sems.at[1], k).start()
        return carry

    lax.fori_loop(0, 8, step, 0)
    for k in range(8):
        chunk_copy(out_v, out, sems.at[1], k).wait()


def finish(got, lin, t):
    return pl.pallas_call(
        finish_body,
        in_specs=[VM, HBM, VM, VM],
        out_specs=HBM,
        out_shape=GRID_ROWS,
        scratch_shapes=[pltpu.VMEM((4096, ZT), BF)] * 2
        + SYNTH_SCRATCH
        + [pltpu.SemaphoreType.DMA((2, 8))],
        name="finish",
        compiler_params=pltpu.CompilerParams(vmem_limit_bytes=52 << 20),
    )(got, lin, t["depth"], t["middle"])


def linear_body(turn, v, matrix, bias, out, have, made, kron, sems):
    for k in range(8):
        chunk_copy(v, have, sems.at[0], k).start()
    rows = lax.broadcasted_iota(jnp.int32, (512, C), 0) // 16
    pick = jnp.where(rows == lax.broadcasted_iota(jnp.int32, (512, C), 1), 1.0, 0.0).astype(BF)
    if turn:
        wide = lax.dot_general(matrix[...], pick, (((0,), (1,)), ((), ())), preferred_element_type=F32)
    else:
        wide = dot_t(matrix[...], pick)
    tall = dot(pick, wide.astype(BF))
    row = lax.broadcasted_iota(jnp.int32, (512, 512), 0) % 16
    col = lax.broadcasted_iota(jnp.int32, (512, 512), 1) % 16
    kron[...] = jnp.where(row == col, tall * 0.5, 0.0).astype(BF)
    for x in range(2):
        for k in range(4):
            chunk_copy(v, have, sems.at[0], x * 4 + k).wait()
        grid = have.at[pl.ds(x * 2048, 2048)].reshape(C, Y, ZT)
        done = made.at[pl.ds(x * 2048, 2048)].reshape(C, Y, ZT)
        for g in range(4):
            cells = grid[:, g * 16 : g * 16 + 16, :].reshape(512, ZT)
            result = dot(kron[...], cells)
            for c in range(C):
                one = result[c * 16 : c * 16 + 16]
                if bias is not None:
                    one = one + 0.5 * bias[c]
                done[c, g * 16 : g * 16 + 16, :] = one.astype(BF)
        for k in range(4):
            chunk_copy(made, out, sems.at[1], x * 4 + k).start()
    for k in range(8):
        chunk_copy(made, out, sems.at[1], k).wait()


def linear(values, matrix, bias, turn):
    if bias is None:
        body = lambda v, m, *rest: linear_body(turn, v, m, None, *rest)
        more = []
    else:
        body = partial(linear_body, turn)
        more = [bias]
    return pl.pallas_call(
        body,
        in_specs=[HBM, VM] + [pl.BlockSpec(memory_space=pltpu.SMEM)] * len(more),
        out_specs=HBM,
        out_shape=GRID_ROWS,
        scratch_shapes=[
            pltpu.VMEM((4096, ZT), BF), pltpu.VMEM((4096, ZT), BF), pltpu.VMEM((512, 512), BF),
            pltpu.SemaphoreType.DMA((2, 8)),
        ],
        name="linear",
        compiler_params=pltpu.CompilerParams(vmem_limit_bytes=52 << 20),
    )(values, matrix, *more)


def weight_body(*refs):
    specs, grads = refs[:2], refs[2:4]
    fold, out, srow, grow, made, sem = refs[4:]
    for i in range(2):
        srow[i * 2 : i * 2 + 2] = specs[i][...].astype(F32)
        grow[i * 2 : i * 2 + 2] = grads[i][...].astype(F32)

    mask = mode_mask()
    low = lax.broadcasted_iota(jnp.int32, (32, 128), 1) < 64
    blank = jnp.zeros((64, 128), F32)

    def tall(ref, q, s, k, h):
        row = ref[s, q, k : k + 1, h * 256 : h * 256 + 256]
        return jnp.where(mask, jnp.broadcast_to(row, (8, 256)), 0.0)

    def copy_out(q):
        return pltpu.make_async_copy(made.at[q], out.at[q], sem.at[q])

    def step(q, carry):
        for h in range(2):
            sides = [
                jnp.concatenate(
                    [tall(grow, q, s, p * 16 + kx, h) for kx in range(MX) for s in range(4)], axis=0
                ).astype(BF)
                for p in range(2)
            ]
            pair = dot(jnp.concatenate(sides, axis=1), fold[...])
            for group in range(4):
                left = [
                    tall(srow, q, s, p * 16 + group * 4 + j, h)
                    for j in range(4)
                    for p in range(2)
                    for s in range(4)
                ]
                left = jnp.concatenate(left, axis=0).astype(BF)
                blocks = []
                for j in range(4):
                    at = (group * 4 + j) * 32
                    here = pair[at : at + 32]
                    there = jnp.concatenate([here[:, 64:], here[:, :64]], axis=1)
                    if j % 2 == 0:
                        one, two = jnp.where(low, here, 0.0), jnp.where(low, there, 0.0)
                    else:
                        one, two = jnp.where(low, 0.0, there), jnp.where(low, 0.0, here)
                    piece = jnp.concatenate([one, two], axis=0)
                    blocks.append(jnp.concatenate([piece, blank] if j < 2 else [blank, piece], axis=1))
                right = jnp.concatenate(blocks, axis=0).astype(BF)
                grad = lax.dot_general(
                    left, right, (((0,), (0,)), ((), ())), preferred_element_type=F32
                )
                for j in range(4):
                    at = group * 2048 + (j * 2 + h) * 256
                    made[q, at : at + 256, :] = grad[:, j * 64 : j * 64 + 64]
        copy_out(q).start()
        return carry

    lax.fori_loop(0, NQ, step, 0)
    for q in range(NQ):
        copy_out(q).wait()


def weight_gradient(specs, grads, t):
    return pl.pallas_call(
        weight_body,
        in_specs=[VM] * 5,
        out_specs=HBM,
        out_shape=jax.ShapeDtypeStruct((NQ, 8192, 64), F32),
        scratch_shapes=[pltpu.VMEM((4, NQ, 32, 512), F32), pltpu.VMEM((4, NQ, 32, 512), F32)]
        + [pltpu.VMEM((NQ, 8192, 64), F32), pltpu.SemaphoreType.DMA((NQ,))],
        name="weight_gradient",
        compiler_params=pltpu.CompilerParams(vmem_limit_bytes=52 << 20),
    )(*specs, *grads, t["fold"])


def exchange(values):
    return lax.all_to_all(values, "slab", split_axis=0, concat_axis=0, tiled=True)


def far_chip(values):
    return lax.ppermute(values, "dp", [(i, i ^ 2) for i in range(4)])


def everyone(values, far):
    both = jnp.stack([values, far])
    near = lax.ppermute(both, "dp", [(i, i ^ 1) for i in range(4)])
    return both, near


def layer(field, cotangent, spectral_weight, point_weight, bias_term):
    t = tables()
    rows = field.reshape(4096, ZT)
    weights = spectral_weight.reshape(NQ, 8192, 64)
    sent = exchange(analyse(rows, t))
    lin = linear(rows, point_weight, bias_term, False)
    sent, lin = lax.optimization_barrier((sent, lin))
    back, spec = mix_forward(sent, weights, t)
    got = exchange(back)
    got, spec = lax.optimization_barrier((got, spec))
    far = far_chip(spec)
    act, grad_pre, out = activate(got, lin, cotangent.reshape(4096, ZT), t)
    out, spec, far = lax.optimization_barrier((out, spec, far))
    sent = exchange(out)
    lin = linear(grad_pre, point_weight, None, True)
    sent, lin = lax.optimization_barrier((sent, lin))
    back, grad_spec = mix_backward(sent, weights, t)
    far_grad = far_chip(grad_spec)
    got = exchange(back)
    specs = everyone(spec, far)
    grads = everyone(grad_spec, far_grad)
    weight_grad = weight_gradient(specs, grads, t).reshape(NQ, MX, MY, C, 2 * C)
    got, weight_grad = lax.optimization_barrier((got, weight_grad))
    total = finish(got, lin, t)
    shape = (1, 2, C, Y, ZT)
    return act.reshape(shape), total.reshape(shape), weight_grad


def solution(mesh):
    placed = (
        P("dp", "slab", None, None, None),
        P("dp", "slab", None, None, None),
        P("slab", None, None, None, None),
        P(),
        P(),
    )
    return jax.shard_map(
        layer,
        mesh=mesh,
        in_specs=placed,
        out_specs=(
            P("dp", "slab", None, None, None),
            P("dp", "slab", None, None, None),
            P("slab", None, None, None, None),
        ),
        check_vma=False,
    )
```

```python
import math
from functools import partial

import jax
import jax.numpy as jnp
import numpy as np
from jax import lax
from jax.experimental import pallas as pl
from jax.experimental.pallas import tpu as pltpu
from jax.sharding import PartitionSpec as P


X = 64
Y = 64
Z = 32
T_SIZE = 16
ZT = Z * T_SIZE
C = 32
MX = 16
MY = 16
MZ = 12
MT = 8
NQ = 3
ND = 32
SCALE = 1.0 / (X * Y * Z * T_SIZE)
BF = jnp.bfloat16
F32 = jnp.float32


def signed(modes):
    i = np.arange(modes)
    return np.where(i < modes // 2, i, i - modes)


def inner_np():
    q = np.arange(MZ * MT)
    place = np.arange(ZT)
    kz = (signed(MZ)[q // MT] % Z)[:, None]
    kt = (q % MT)[:, None]
    counts = kz * (place // T_SIZE)[None] % Z * T_SIZE + kt * (place % T_SIZE)[None] % T_SIZE * Z
    angle = 2.0 * math.pi / ZT * (counts % ZT)
    return np.stack([np.cos(angle), -np.sin(angle)]).astype(np.float32)


def complex_np(modes, length):
    k = (signed(modes) % length)[:, None]
    angle = 2.0 * math.pi / length * (k * np.arange(length)[None] % length)
    c, s = np.cos(angle), np.sin(angle)
    return np.stack([np.stack([c, s], 1), np.stack([-s, c], 1)]).astype(np.float32)


def tables():
    inner = inner_np()
    mid = complex_np(MY, Y)
    out = complex_np(MX, X)
    depth = np.zeros((2, 128, ZT), np.float32)
    depth[:, :96] = inner.reshape(2, ND, NQ, ZT).transpose(0, 2, 1, 3).reshape(2, 96, ZT)
    depth = depth.reshape(256, ZT)
    middle = np.einsum("rkpy,cd->pcyrkd", mid, np.eye(8, dtype=np.float32)).reshape(1024, 256)
    eye4 = np.eye(4, dtype=np.float32)
    ana_out = np.einsum("rkpsi,gh->grkspih", out.reshape(2, MX, 2, ND, 2), eye4).reshape(128, 512)
    syn_out = out.reshape(2, MX, 2, ND, 2).transpose(2, 4, 3, 0, 1)
    fwd_out = np.repeat(syn_out.reshape(128, 32), 16, axis=1)
    bwd_out = np.repeat(syn_out.reshape(128, 32), 8, axis=1)
    spread = np.zeros((2, 2, 4, 8, 4, MY, 8), np.float32)
    for g in range(4):
        for c in range(8):
            spread[0, 0, g, c, g, :, c] = 1.0
            spread[1, 1, g, c, g, :, c] = 1.0
    spread = spread.reshape(2, 64, 512)
    fold = np.zeros((2, 8, C, 128), np.float32)
    for o in range(C):
        fold[0, :, o, o] = 1.0
        fold[0, :, o, 96 + o] = -1.0
        fold[1, :, o, 32 + o] = 1.0
        fold[1, :, o, 64 + o] = 1.0
    fold = fold.reshape(512, 128)
    t = dict(
        depth=depth, middle=middle, ana_out=ana_out, fwd_out=fwd_out * (SCALE / 2.0), bwd_out=bwd_out,
        spread=spread, fold=fold,
    )
    return {k: jnp.asarray(v, BF) for k, v in t.items()}


def dot(a, b):
    return lax.dot_general(a, b, (((1,), (0,)), ((), ())), preferred_element_type=F32)


def dot_t(a, b):
    return lax.dot_general(a, b, (((1,), (1,)), ((), ())), preferred_element_type=F32)


def owner_table(depth):
    return jnp.concatenate([depth[0:96, :], depth[128:224, :]], axis=0)


def analyse_rows(rows, slot, table, first):
    part = dot_t(table, rows).astype(BF)
    at = pl.ds(slot * 96, 96) if isinstance(slot, int) else pl.ds(pl.multiple_of(slot * 96, 32), 96)
    first[at, 0:512] = part[:96]
    first[at, 512:1024] = part[96:]


def by_owner(first, middle, out, work):
    second = dot(first[...], middle[...])
    for slot in range(8):
        for qi in range(NQ):
            for r in range(2):
                at = slot * 96 + qi * 32
                work[qi, pl.ds(r * 8 + slot, ND, stride=16), :] = second[
                    at : at + 32, r * 128 : r * 128 + 128
                ]
    for qi in range(NQ):
        out[:, qi * 16 : qi * 16 + 16, :] = work[qi].reshape(ND, 16, 128).astype(BF)


def chunk_copy(src, dst, sem, k):
    at = pl.ds(k * 512, 512)
    return pltpu.make_async_copy(src.at[at], dst.at[at], sem.at[k])


def analyse_body(v, depth_h, middle_h, out, have, first, work, depth, middle, sem, more):
    tables_in = [
        pltpu.make_async_copy(depth_h, depth, more.at[0]),
        pltpu.make_async_copy(middle_h, middle, more.at[1]),
    ]
    tables_in[0].start()
    for k in range(8):
        chunk_copy(v, have, sem, k).start()
    tables_in[1].start()
    tables_in[0].wait()
    table = owner_table(depth)
    for half in range(2):
        for k in range(half * 4, half * 4 + 4):
            chunk_copy(v, have, sem, k).wait()
        part = dot_t(table, have[half * 2048 : half * 2048 + 2048, :]).astype(BF)
        for k in range(4):
            at = half * 384 + k * 96
            first[at : at + 96, 0:512] = part[:96, k * 512 : k * 512 + 512]
            first[at : at + 96, 512:1024] = part[96:, k * 512 : k * 512 + 512]
    tables_in[1].wait()
    by_owner(first, middle, out, work)


HBM = pl.BlockSpec(memory_space=pltpu.HBM)
VM = pl.BlockSpec(memory_space=pltpu.VMEM)
GRID_ROWS = jax.ShapeDtypeStruct((4096, ZT), BF)
SENT = jax.ShapeDtypeStruct((ND, 48, 128), BF)


def analyse(values, t):
    return pl.pallas_call(
        analyse_body,
        in_specs=[HBM, HBM, HBM],
        out_specs=VM,
        out_shape=SENT,
        scratch_shapes=[
            pltpu.VMEM((4096, ZT), BF), pltpu.VMEM((768, 1024), BF),
            pltpu.VMEM((NQ, 512, 128), F32), pltpu.VMEM((256, ZT), BF), pltpu.VMEM((1024, 256), BF),
            pltpu.SemaphoreType.DMA((8,)), pltpu.SemaphoreType.DMA((2,)),
        ],
        name="analyse",
        compiler_params=pltpu.CompilerParams(vmem_limit_bytes=60 << 20),
    )(values, t["depth"], t["middle"])


def channel_order(perm):
    row = lax.broadcasted_iota(jnp.int32, (512, 512), 0)
    col = lax.broadcasted_iota(jnp.int32, (512, 512), 1)
    place = row // 8 % 16 * 32 + row // 128 * 8 + row % 8
    perm[...] = jnp.where(place == col, 1.0, 0.0).astype(BF)


def spectrum_rows(got, ana_out, perm, scale):
    tall = [got[:, q * 16 : q * 16 + 16, :].reshape(512, 128) for q in range(NQ)]
    parts = dot(ana_out[...], jnp.concatenate(tall, axis=1))
    if scale is not None:
        parts = parts * scale
    parts = parts.astype(BF)
    rows = [
        jnp.concatenate([parts[g * 32 : g * 32 + 32, q * 128 : q * 128 + 128] for g in range(4)], axis=1)
        for q in range(NQ)
    ]
    return dot(jnp.concatenate(rows, axis=0), perm[...])


def mode_mask():
    lane = lax.broadcasted_iota(jnp.int32, (8, 256), 1) // 32
    return lane == lax.broadcasted_iota(jnp.int32, (8, 256), 0)


def scatter_owner(synth, q, work, out):
    for r in range(2):
        for xi in range(2):
            for g in range(4):
                at = (r * 2 + xi) * 32
                work[q, pl.ds(r * 8 + xi * 4 + g, ND, stride=16), :] = synth[
                    at : at + 32, g * 128 : g * 128 + 128
                ]
    out[:, q * 16 : q * 16 + 16, :] = work[q].reshape(ND, 16, 128).astype(BF)


def weight_copy(w, have, sem, q):
    return pltpu.make_async_copy(w.at[q], have.at[q], sem.at[q])


def mix_forward_body(
    got, w, ana_out, spread, fwd_out, out, spec, have, srow, mixed, work, perm, sem
):
    for q in range(NQ):
        weight_copy(w, have, sem, q).start()
    channel_order(perm)
    rows = spectrum_rows(got, ana_out, perm, None)
    srow[...] = rows
    for q in range(NQ):
        spec[q] = rows[q * 32 : q * 32 + 32].astype(BF)
    mask = mode_mask()
    row_ky = lax.broadcasted_iota(jnp.int32, (256, 512), 0) % 16
    lane_ky = lax.broadcasted_iota(jnp.int32, (256, 512), 1) // 8 % 16
    same = row_ky == lane_ky
    for q in range(NQ):
        weight_copy(w, have, sem, q).wait()
        for kx in range(MX):
            for h in range(2):
                lanes = slice(h * 256, h * 256 + 256)
                at = q * 32 + kx
                real = jnp.where(mask, jnp.broadcast_to(srow[at : at + 1, lanes], (8, 256)), 0.0)
                at = at + 16
                imag = jnp.where(mask, jnp.broadcast_to(srow[at : at + 1, lanes], (8, 256)), 0.0)
                left = jnp.concatenate([real, imag], axis=0).astype(BF)
                at = (kx * 2 + h) * 256
                both = dot(left, have[q, at : at + 256, :])
                low = both[8:16]
                turned = jnp.concatenate([-low[:, 32:], low[:, :32]], axis=1)
                at = kx * 16 + h * 8
                mixed[q, at : at + 8, :] = both[:8] + turned
        values = mixed[q].astype(BF)
        wide = [jnp.where(same, dot(values, spread[p]), 0.0).astype(BF) for p in range(2)]
        synth = dot(fwd_out[...], jnp.concatenate(wide, axis=0))
        scatter_owner(synth, q, work, out)


SPECTRUM = jax.ShapeDtypeStruct((NQ, 32, 512), BF)


def mix_forward(got, weights, t):
    return pl.pallas_call(
        mix_forward_body,
        in_specs=[VM, HBM, VM, VM, VM],
        out_specs=[VM, VM],
        out_shape=[SENT, SPECTRUM],
        scratch_shapes=[
            pltpu.VMEM((NQ, 8192, 64), BF), pltpu.VMEM((96, 512), F32), pltpu.VMEM((NQ, 256, 64), F32),
            pltpu.VMEM((NQ, 512, 128), F32), pltpu.VMEM((512, 512), BF),
            pltpu.SemaphoreType.DMA((NQ,)),
        ],
        name="mix_forward",
        compiler_params=pltpu.CompilerParams(vmem_limit_bytes=52 << 20),
    )(got, weights, t["ana_out"], t["spread"], t["fwd_out"])


def mix_backward_body(
    got, w, ana_out, fold, bwd_out, out, spec, have, srow, pair, masked, work, perm, sem
):
    for q in range(NQ):
        weight_copy(w, have, sem, q).start()
    channel_order(perm)
    rows = spectrum_rows(got, ana_out, perm, SCALE / 2.0)
    srow[...] = rows
    for q in range(NQ):
        spec[q] = rows[q * 32 : q * 32 + 32].astype(BF)
    mask = mode_mask()
    for h in range(2):
        lanes = slice(h * 256, h * 256 + 256)
        sides = []
        for part in range(2):
            tall = [
                jnp.where(mask, jnp.broadcast_to(srow[k : k + 1, lanes], (8, 256)), 0.0)
                for q in range(NQ)
                for k in range(q * 32 + part * 16, q * 32 + part * 16 + 16)
            ]
            sides.append(jnp.concatenate(tall, axis=0).astype(BF))
        pair[h] = dot(jnp.concatenate(sides, axis=1), fold[...])
    for q in range(NQ):
        weight_copy(w, have, sem, q).wait()
        for kx in range(MX):
            for h in range(2):
                at = q * 128 + kx * 8
                both = pair[h, at : at + 8, :]
                left = jnp.concatenate([both[:, :64], both[:, 64:]], axis=0).astype(BF)
                at = (kx * 2 + h) * 256
                full = dot_t(left, have[q, at : at + 256, :])
                masked[q, h, kx * 8 : kx * 8 + 8, :] = jnp.where(mask, full[:8], 0.0)
                masked[q, h, 128 + kx * 8 : 136 + kx * 8, :] = jnp.where(mask, full[8:], 0.0)
        synth = [dot(bwd_out[...], masked[q, h].astype(BF)).astype(BF) for h in range(2)]
        turned = dot_t(jnp.concatenate(synth, axis=1), perm[...])
        scatter_owner(turned, q, work, out)


def mix_backward(got, weights, t):
    return pl.pallas_call(
        mix_backward_body,
        in_specs=[VM, HBM, VM, VM, VM],
        out_specs=[VM, VM],
        out_shape=[SENT, SPECTRUM],
        scratch_shapes=[
            pltpu.VMEM((NQ, 8192, 64), BF), pltpu.VMEM((96, 512), F32), pltpu.VMEM((2, 384, 128), F32),
            pltpu.VMEM((NQ, 2, 256, 256), F32), pltpu.VMEM((NQ, 512, 128), F32),
            pltpu.VMEM((512, 512), BF), pltpu.SemaphoreType.DMA((NQ,)),
        ],
        name="mix_backward",
        compiler_params=pltpu.CompilerParams(vmem_limit_bytes=52 << 20),
    )(got, weights, t["ana_out"], t["fold"], t["bwd_out"])


def unpack(got, have, turned, middle, tall):
    for qi in range(NQ):
        have[qi] = got[:, qi * 16 : qi * 16 + 16, :].reshape(512, 128).astype(F32)
    for slot in range(8):
        for p in range(2):
            pieces = [have[qi, pl.ds(p * 8 + slot, ND, stride=16), :] for qi in range(NQ)]
            pieces.append(jnp.zeros((ND, 128), F32))
            turned[slot * 128 : slot * 128 + 128, p * 128 : p * 128 + 128] = jnp.concatenate(
                pieces, axis=0
            ).astype(BF)
    for r in range(2):
        block = dot_t(middle[r * 512 : r * 512 + 512, :], turned[...]).astype(BF)
        for slot in range(8):
            tall[slot * 512 : slot * 512 + 512, r * 128 : r * 128 + 128] = block[
                :, slot * 128 : slot * 128 + 128
            ]


ROOT = math.sqrt(2.0 / math.pi)


def activate_body(
    got, lin, cot, depth, middle, act, grad, out, lin_v, cot_v, act_v, grad_v, have, turned, tall,
    first, work, sems,
):
    for k in range(8):
        chunk_copy(lin, lin_v, sems.at[0], k).start()
        chunk_copy(cot, cot_v, sems.at[1], k).start()
    grad_v[0:512, :] = jnp.zeros((512, ZT), BF)
    unpack(got, have, turned, middle, tall)
    table = owner_table(depth)

    def grad_copy(k):
        at = pl.ds(k * 512, 512)
        return pltpu.make_async_copy(grad_v.at[pl.ds(k * 512 + 512, 512)], grad.at[at], sems.at[3, k])

    def step(i, carry):
        base = pl.multiple_of(i * 1024, 1024)
        for u in range(2):
            chunk_copy(lin, lin_v, sems.at[0], i * 2 + u).wait()
            chunk_copy(cot, cot_v, sems.at[1], i * 2 + u).wait()
        for u in range(2):
            rows = grad_v[pl.ds(base + u * 512, 512), :]
            slot = jnp.maximum(i * 2 + u - 1, 0)
            analyse_rows(rows, slot, table, first)
            at = pl.ds(base + u * 512, 512)
            w = dot(tall[at, :], depth[...]) + lin_v[at, :].astype(F32)
            square = w * w
            t = jnp.tanh(w * (2.0 * ROOT + (8.0 * ROOT * 0.044715) * square))
            one = 1.0 + t
            value = w * one
            slope = one + value * (1.0 - t) * (2.0 * ROOT + (24.0 * ROOT * 0.044715) * square)
            act_v[at, :] = value.astype(BF)
            grad_v[pl.ds(base + u * 512 + 512, 512), :] = cot_v[at, :] * slope.astype(BF)
            chunk_copy(act_v, act, sems.at[2], i * 2 + u).start()
            grad_copy(i * 2 + u).start()
        return carry

    lax.fori_loop(0, 4, step, 0)
    analyse_rows(grad_v[4096:4608, :], 7, table, first)
    by_owner(first, middle, out, work)
    for k in range(8):
        chunk_copy(act_v, act, sems.at[2], k).wait()
        grad_copy(k).wait()


SYNTH_SCRATCH = [
    pltpu.VMEM((NQ, 512, 128), F32), pltpu.VMEM((1024, 256), BF), pltpu.VMEM((4096, 256), BF),
]


def activate(got, lin, cot, t):
    return pl.pallas_call(
        activate_body,
        in_specs=[VM, HBM, HBM, VM, VM],
        out_specs=[HBM, HBM, VM],
        out_shape=[GRID_ROWS, GRID_ROWS, SENT],
        scratch_shapes=[pltpu.VMEM((4096, ZT), BF)] * 3
        + [pltpu.VMEM((4608, ZT), BF)]
        + SYNTH_SCRATCH
        + [
            pltpu.VMEM((768, 1024), BF), pltpu.VMEM((NQ, 512, 128), F32),
            pltpu.SemaphoreType.DMA((4, 8)),
        ],
        name="activate",
        compiler_params=pltpu.CompilerParams(vmem_limit_bytes=52 << 20),
    )(got, lin, cot, t["depth"], t["middle"])


def finish_body(got, lin, depth, middle, out, lin_v, out_v, have, turned, tall, sems):
    for k in range(8):
        chunk_copy(lin, lin_v, sems.at[0], k).start()
    unpack(got, have, turned, middle, tall)

    def step(k, carry):
        for u in range(2):
            chunk_copy(lin, lin_v, sems.at[0], k * 2 + u).wait()
        at = pl.ds(pl.multiple_of(k * 1024, 1024), 1024)
        out_v[at, :] = (dot(tall[at, :], depth[...]) + lin_v[at, :].astype(F32)).astype(BF)
        for u in range(2):
            chunk_copy(out_v, out, sems.at[1], k * 2 + u).start()
        return carry

    lax.fori_loop(0, 4, step, 0)
    for k in range(8):
        chunk_copy(out_v, out, sems.at[1], k).wait()


def finish(got, lin, t):
    return pl.pallas_call(
        finish_body,
        in_specs=[VM, HBM, VM, VM],
        out_specs=HBM,
        out_shape=GRID_ROWS,
        scratch_shapes=[pltpu.VMEM((4096, ZT), BF)] * 2
        + SYNTH_SCRATCH
        + [pltpu.SemaphoreType.DMA((2, 8))],
        name="finish",
        compiler_params=pltpu.CompilerParams(vmem_limit_bytes=52 << 20),
    )(got, lin, t["depth"], t["middle"])


def linear_body(turn, v, matrix, bias, out, have, made, kron, sems):
    for k in range(8):
        chunk_copy(v, have, sems.at[0], k).start()
    rows = lax.broadcasted_iota(jnp.int32, (512, C), 0) // 16
    pick = jnp.where(rows == lax.broadcasted_iota(jnp.int32, (512, C), 1), 1.0, 0.0).astype(BF)
    if turn:
        wide = lax.dot_general(matrix[...], pick, (((0,), (1,)), ((), ())), preferred_element_type=F32)
    else:
        wide = dot_t(matrix[...], pick)
    tall = dot(pick, wide.astype(BF))
    row = lax.broadcasted_iota(jnp.int32, (512, 512), 0) % 16
    col = lax.broadcasted_iota(jnp.int32, (512, 512), 1) % 16
    kron[...] = jnp.where(row == col, tall * 0.5, 0.0).astype(BF)
    for x in range(2):
        for k in range(4):
            chunk_copy(v, have, sems.at[0], x * 4 + k).wait()
        grid = have.at[pl.ds(x * 2048, 2048)].reshape(C, Y, ZT)
        done = made.at[pl.ds(x * 2048, 2048)].reshape(C, Y, ZT)
        for g in range(4):
            cells = grid[:, g * 16 : g * 16 + 16, :].reshape(512, ZT)
            result = dot(kron[...], cells)
            for c in range(C):
                one = result[c * 16 : c * 16 + 16]
                if bias is not None:
                    one = one + 0.5 * bias[c]
                done[c, g * 16 : g * 16 + 16, :] = one.astype(BF)
        for k in range(4):
            chunk_copy(made, out, sems.at[1], x * 4 + k).start()
    for k in range(8):
        chunk_copy(made, out, sems.at[1], k).wait()


def linear(values, matrix, bias, turn):
    if bias is None:
        body = lambda v, m, *rest: linear_body(turn, v, m, None, *rest)
        more = []
    else:
        body = partial(linear_body, turn)
        more = [bias]
    return pl.pallas_call(
        body,
        in_specs=[HBM, VM] + [pl.BlockSpec(memory_space=pltpu.SMEM)] * len(more),
        out_specs=HBM,
        out_shape=GRID_ROWS,
        scratch_shapes=[
            pltpu.VMEM((4096, ZT), BF), pltpu.VMEM((4096, ZT), BF), pltpu.VMEM((512, 512), BF),
            pltpu.SemaphoreType.DMA((2, 8)),
        ],
        name="linear",
        compiler_params=pltpu.CompilerParams(vmem_limit_bytes=52 << 20),
    )(values, matrix, *more)


def weight_body(*refs):
    specs, grads = refs[:2], refs[2:4]
    fold, out, srow, grow, made, sem = refs[4:]
    for i in range(2):
        srow[i * 2 : i * 2 + 2] = specs[i][...].astype(F32)
        grow[i * 2 : i * 2 + 2] = grads[i][...].astype(F32)

    mask = mode_mask()
    low = lax.broadcasted_iota(jnp.int32, (32, 128), 1) < 64
    blank = jnp.zeros((64, 128), F32)

    def tall(ref, q, s, k, h):
        row = ref[s, q, k : k + 1, h * 256 : h * 256 + 256]
        return jnp.where(mask, jnp.broadcast_to(row, (8, 256)), 0.0)

    def copy_out(q):
        return pltpu.make_async_copy(made.at[q], out.at[q], sem.at[q])

    def step(q, carry):
        for h in range(2):
            sides = [
                jnp.concatenate(
                    [tall(grow, q, s, p * 16 + kx, h) for kx in range(MX) for s in range(4)], axis=0
                ).astype(BF)
                for p in range(2)
            ]
            pair = dot(jnp.concatenate(sides, axis=1), fold[...])
            for group in range(4):
                left = [
                    tall(srow, q, s, p * 16 + group * 4 + j, h)
                    for j in range(4)
                    for p in range(2)
                    for s in range(4)
                ]
                left = jnp.concatenate(left, axis=0).astype(BF)
                blocks = []
                for j in range(4):
                    at = (group * 4 + j) * 32
                    here = pair[at : at + 32]
                    there = jnp.concatenate([here[:, 64:], here[:, :64]], axis=1)
                    if j % 2 == 0:
                        one, two = jnp.where(low, here, 0.0), jnp.where(low, there, 0.0)
                    else:
                        one, two = jnp.where(low, 0.0, there), jnp.where(low, 0.0, here)
                    piece = jnp.concatenate([one, two], axis=0)
                    blocks.append(jnp.concatenate([piece, blank] if j < 2 else [blank, piece], axis=1))
                right = jnp.concatenate(blocks, axis=0).astype(BF)
                grad = lax.dot_general(
                    left, right, (((0,), (0,)), ((), ())), preferred_element_type=F32
                )
                for j in range(4):
                    at = group * 2048 + (j * 2 + h) * 256
                    made[q, at : at + 256, :] = grad[:, j * 64 : j * 64 + 64]
        copy_out(q).start()
        return carry

    lax.fori_loop(0, NQ, step, 0)
    for q in range(NQ):
        copy_out(q).wait()


def weight_gradient(specs, grads, t):
    return pl.pallas_call(
        weight_body,
        in_specs=[VM] * 5,
        out_specs=HBM,
        out_shape=jax.ShapeDtypeStruct((NQ, 8192, 64), F32),
        scratch_shapes=[pltpu.VMEM((4, NQ, 32, 512), F32), pltpu.VMEM((4, NQ, 32, 512), F32)]
        + [pltpu.VMEM((NQ, 8192, 64), F32), pltpu.SemaphoreType.DMA((NQ,))],
        name="weight_gradient",
        compiler_params=pltpu.CompilerParams(vmem_limit_bytes=52 << 20),
    )(*specs, *grads, t["fold"])


def exchange(values):
    return lax.all_to_all(values, "slab", split_axis=0, concat_axis=0, tiled=True)


def far_chip(values):
    return lax.ppermute(values, "dp", [(i, i ^ 2) for i in range(4)])


def everyone(values, far):
    both = jnp.stack([values, far])
    near = lax.ppermute(both, "dp", [(i, i ^ 1) for i in range(4)])
    return both, near


def layer(field, cotangent, spectral_weight, point_weight, bias_term):
    t = tables()
    rows = field.reshape(4096, ZT)
    weights = spectral_weight.reshape(NQ, 8192, 64)
    sent = exchange(analyse(rows, t))
    lin = linear(rows, point_weight, bias_term, False)
    sent, lin = lax.optimization_barrier((sent, lin))
    back, spec = mix_forward(sent, weights, t)
    got = exchange(back)
    got, spec = lax.optimization_barrier((got, spec))
    far = far_chip(spec)
    act, grad_pre, out = activate(got, lin, cotangent.reshape(4096, ZT), t)
    out, spec, far = lax.optimization_barrier((out, spec, far))
    sent = exchange(out)
    lin = linear(grad_pre, point_weight, None, True)
    sent, lin = lax.optimization_barrier((sent, lin))
    back, grad_spec = mix_backward(sent, weights, t)
    far_grad = far_chip(grad_spec)
    got = exchange(back)
    specs = everyone(spec, far)
    grads = everyone(grad_spec, far_grad)
    weight_grad = weight_gradient(specs, grads, t).reshape(NQ, MX, MY, C, 2 * C)
    got, weight_grad = lax.optimization_barrier((got, weight_grad))
    total = finish(got, lin, t)
    shape = (1, 2, C, Y, ZT)
    return act.reshape(shape), total.reshape(shape), weight_grad


def solution(mesh):
    placed = (
        P("dp", "slab", None, None, None),
        P("dp", "slab", None, None, None),
        P("slab", None, None, None, None),
        P(),
        P(),
    )
    return jax.shard_map(
        layer,
        mesh=mesh,
        in_specs=placed,
        out_specs=(
            P("dp", "slab", None, None, None),
            P("dp", "slab", None, None, None),
            P("slab", None, None, None, None),
        ),
        check_vma=False,
    )
```
